32 devices in a mesh: tile: 8 (over z, y), clip: 4 (over x, core).
Axes of the slice: x: 2, y: 2, z: 4, core: 2. Of those that a mesh axis runs over, the one named last changes fastest.
Arguments:
- seq_rows: bfloat16 [32768, 512], P(('tile', 'clip'))
- plan_owner: int32 [32768], P(('tile', 'clip')), may hold values from 0 to 31, as said below
- plan_slot: int32 [32768], P(('tile', 'clip')), may hold values from 0 to 1023, as said below
- live_frames: int32 [4], replicated, may hold values from 1 to 4, as said below
- norm_gain: float32 [512], replicated, may hold values from 0.1 to 1.9
- norm_bias: float32 [512], replicated, may hold values from -3 to 3
- conv_weight: bfloat16 [3, 3, 512, 3, 256], replicated, may hold values from -0.0546875 to 0.0546875
- conv_bias: float32 [256], replicated, may hold values from -3 to 3
Outputs:
- decoded: bfloat16 [4, 8, 4, 8, 32, 256], P('clip', 'tile')
The draws below stay inside these ranges and needn't reach their ends.
Inputs may be any that keep to these rules, and one draw needn't show every extreme that they name: `plan_owner`: owner o is tile o % 8 of clip o // 8. The 1024 rows of each device send 32 // 2 or 48 rows to each owner, so at most 48, which is reached. The pairs of plan_owner and plan_slot are all distinct: every slot of every owner receives exactly one row. `live_frames`: some clip has all 4 frames live.
All inputs are finite; a program needn't handle non-finite values.
Results may differ from the reference program's by a relative error of at most 0.004.
Values may be sent and summed in bfloat16 or wider, within the bound.
A program may use at most 128 MiB of HBM per device.

```python
import math
import jax
import jax.numpy as jnp
from jax import lax

C = 512
CO = 256
GROUPS = 32
LT = 4
TH = 8
TW = 32
GW = 4
TILES = 8
CLIPS = 4
OWNERS = 32
ROWS_DEV = 1024
PER = 32
SEQ = 32768


def plan_tables(key):
    base = jax.random.fold_in(key, 17)
    key_first, key_second, key_slots, key_order = jax.random.split(base, 4)
    first = jax.random.permutation(key_first, OWNERS)
    second = jax.random.permutation(key_second, OWNERS)
    pattern = (first[:, None] + second[None, :]) % OWNERS < OWNERS // 2
    counts = PER // 2 + PER * pattern.astype(jnp.int32)
    ends = jnp.cumsum(counts, axis=1)
    starts = ends - counts
    position = jnp.arange(ROWS_DEV, dtype=jnp.int32)
    owner_of = jax.vmap(lambda row_ends: jnp.searchsorted(row_ends, position, side='right'))(ends).astype(jnp.int32)
    ranking = position[None, :] - jnp.take_along_axis(starts, owner_of, axis=1)
    earlier = jnp.cumsum(counts, axis=0) - counts
    linear = jnp.take_along_axis(earlier, owner_of, axis=1) + ranking
    shuffles = jax.vmap(lambda single: jax.random.permutation(single, ROWS_DEV))(jax.random.split(key_slots, OWNERS)).astype(jnp.int32)
    slots = shuffles[owner_of, linear]
    orders = jax.vmap(lambda single: jax.random.permutation(single, ROWS_DEV))(jax.random.split(key_order, OWNERS)).astype(jnp.int32)
    owner_final = jnp.take_along_axis(owner_of, orders, axis=1)
    slot_final = jnp.take_along_axis(slots, orders, axis=1)
    return (owner_final.reshape(-1).astype(jnp.int32), slot_final.reshape(-1).astype(jnp.int32))


def draw_plan_owner(key, part):
    return plan_tables(key)[0]


def draw_plan_slot(key, part):
    return plan_tables(key)[1]


def draw_live_frames(key, part):
    drawn = jax.random.randint(jax.random.fold_in(key, 3), (CLIPS,), 1, LT + 1)
    chosen = jax.random.randint(jax.random.fold_in(key, 5), (), 0, CLIPS)
    return jnp.where(jnp.arange(CLIPS) == chosen, LT, drawn).astype(jnp.int32)


def draw_seq_rows(key, part):
    owners, slots = plan_tables(key)
    tile_of = (owners % TILES).astype(jnp.float32)
    key_noise, key_scale = jax.random.split(jax.random.fold_in(key, 29), 2)
    ramp = tile_of / max(TILES - 1, 1)
    noise = jnp.clip(jax.random.normal(key_noise, (SEQ, C)), -6.0, 6.0)
    channel_scale = jnp.exp(jax.random.uniform(key_scale, (C,)) * math.log(10.0))
    row_scale = 1.0 + 2.0 * ramp
    values = noise * channel_scale[None, :] * row_scale[:, None]
    return values.astype(jnp.float32).astype(jnp.bfloat16)


def gaussian(stream_key, shape, scale, bound, kind=jnp.bfloat16):
    values = scale * jax.random.normal(stream_key, shape, jnp.float32)
    return jnp.clip(values, min=-bound, max=bound).astype(kind)


def setup_inputs(seed: int = 0) -> dict:
    splits = jax.random.split(jax.random.key(seed), 9)
    return {
        "seq_rows": draw_seq_rows(jax.random.fold_in(splits[8], 71), 0),
        "plan_owner": draw_plan_owner(jax.random.fold_in(splits[8], 71), 0),
        "plan_slot": draw_plan_slot(jax.random.fold_in(splits[8], 71), 0),
        "live_frames": draw_live_frames(jax.random.fold_in(splits[8], 71), 0),
        "norm_gain": jnp.clip(1.0 + 0.18 * jax.random.normal(splits[4], (C,), jnp.float32), 0.1, 1.9),
        "norm_bias": gaussian(splits[5], (C,), 0.5, 3.0, jnp.float32),
        "conv_weight": gaussian(splits[6], (3, 3, C, 3, CO), (27 * C) ** -0.5, 0.0546875),
        "conv_bias": gaussian(splits[7], (CO,), 0.5, 3.0, jnp.float32),
    }


EPSILON = 1e-06

def reference(seq_rows, plan_owner, plan_slot, live_frames, norm_gain, norm_bias, conv_weight, conv_bias):
    channels = seq_rows.shape[1]
    out_width = conv_bias.shape[0]
    grid_rows = TILES // GW
    height = grid_rows * TH
    width_cells = GW * TW
    per_group = channels // GROUPS
    flat_index = (plan_owner * ROWS_DEV + plan_slot).astype(jnp.int32)
    placed = jnp.zeros((CLIPS * TILES * ROWS_DEV, channels), jnp.bfloat16).at[flat_index].set(seq_rows)
    placed = placed.reshape(CLIPS, grid_rows, GW, LT, TH, TW, channels)
    volume = placed.transpose(0, 3, 1, 4, 2, 5, 6).reshape(CLIPS, LT, height, width_cells, channels)
    kernel = conv_weight.astype(jnp.float32).transpose(0, 1, 3, 2, 4)

    def one_clip(item):
        clip_volume, frames = item
        values = clip_volume.astype(jnp.float32)
        live_frame = jnp.arange(LT) < frames
        live_weight = live_frame.astype(jnp.float32)[:, None, None, None]
        first_sum = lax.optimization_barrier(jnp.sum(values * live_weight, axis=(0, 1, 2))).reshape(GROUPS, per_group).sum(axis=1)
        second_sum = lax.optimization_barrier(jnp.sum(values * values * live_weight, axis=(0, 1, 2))).reshape(GROUPS, per_group).sum(axis=1)
        count_clip = per_group * frames.astype(jnp.float32) * (height * width_cells)
        mean_group = first_sum / count_clip
        scale_group = lax.rsqrt(second_sum / count_clip - mean_group * mean_group + EPSILON)
        mean_channel = jnp.repeat(mean_group, per_group)
        scale_channel = jnp.repeat(scale_group, per_group)
        normed = (values - mean_channel) * scale_channel * norm_gain + norm_bias
        activation = jax.nn.silu(normed).astype(jnp.bfloat16)
        mixed = lax.conv_general_dilated(activation.astype(jnp.float32)[None], kernel, (1, 1, 1), ((2, 0), (1, 1), (1, 1)), dimension_numbers=('NDHWC', 'DHWIO', 'NDHWC'), precision=lax.Precision.HIGHEST)[0]
        mixed = jnp.where(live_frame[:, None, None, None], mixed + conv_bias, 0.0)
        return mixed.astype(jnp.bfloat16)
    results = lax.map(one_clip, (volume, live_frames))
    results = results.reshape(CLIPS, LT, grid_rows, TH, GW, TW, out_width)
    results = results.transpose(0, 2, 4, 1, 3, 5, 6)
    return results.reshape(CLIPS, TILES, LT, TH, TW, out_width)
```

```python
import functools

import jax
import jax.numpy as jnp
from jax import lax
from jax.experimental import pallas as pl
from jax.experimental.pallas import tpu as pltpu
from jax.sharding import PartitionSpec as P

GROUPS = 32
LT = 4
TH = 8
TW = 32
GW = 4
PLANE = TH * TW
LANES = 128
STAT = 64
EDGE = 2 * LT * TH
EPSILON = 1e-06
HIGHEST = lax.Precision.HIGHEST
F32 = jnp.float32
BF16 = jnp.bfloat16
NT = (((1,), (1,)), ((), ()))
MESH = pl.DeviceIdType.MESH
EDGES = ((0, 1), (0, -1), (1, 0), (-1, 0), (1, 1), (1, -1), (-1, 1), (-1, -1))


def iota(shape, axis):
    return lax.broadcasted_iota(jnp.int32, shape, axis)


def bits(n):
    return n.bit_length() - 1


def dot(a, b, **kw):
    return jnp.dot(a, b, preferred_element_type=F32, **kw)


def joint_of(count, cap):
    joint = max(1, min(count // 4, 256 // cap))
    while (count // 4) % joint:
        joint -= 1
    return joint


def decode_kernel(
    tiles,
    clips,
    cap,
    live_hbm,
    owner_hbm,
    slot_hbm,
    rows_hbm,
    gain_hbm,
    bias_hbm,
    out_bias_hbm,
    weight_hbm,
    out_ref,
    live_ref,
    owner_ref,
    slot_ref,
    rows_ref,
    gain_ref,
    bias_ref,
    out_bias_ref,
    weight_ref,
    send_rows,
    recv_rows,
    send_meta,
    recv_meta,
    slots_ref,
    placed_ref,
    volume,
    side,
    edge_out,
    edge_in,
    face_out,
    face_in,
    corner_out,
    corner_in,
    summed,
    loaded,
    weight_loaded,
    row_sent,
    row_got,
    meta_sent,
    meta_got,
    halo_sent,
    halo_got,
):
    loads = [
        pltpu.make_async_copy(source, target, loaded.at[i])
        for i, (source, target) in enumerate(
            (
                (owner_hbm, owner_ref),
                (slot_hbm, slot_ref),
                (live_hbm, live_ref),
                (rows_hbm, rows_ref),
                (gain_hbm, gain_ref),
                (bias_hbm, bias_ref),
                (out_bias_hbm, out_bias_ref),
            )
        )
    ]
    for load in loads:
        load.start()
    rows, channels = rows_ref.shape
    out_width = out_bias_ref.shape[1]
    weight_loads = [
        pltpu.make_async_copy(
            weight_hbm.at[a * 3 + b, pl.ds(d * channels, channels)],
            weight_ref.at[b, pl.ds(a * channels, channels), pl.ds(d * out_width, out_width)],
            weight_loaded.at[(a * 3 + b) * 3 + d],
        )
        for a in range(3)
        for b in range(3)
        for d in range(3)
    ]
    count = tiles * clips
    depth = bits(count)
    half = count // 2
    quarter = count // 4
    own = half
    my_tile = lax.axis_index("tile")
    my_clip = lax.axis_index("clip")
    me = my_tile * clips + my_clip
    far = me // half
    odd = (me // quarter) % 2

    def other(mask):
        to = 0
        for i in range(depth):
            bit = 1 << i
            to = to + ((me // bit + mask // bit) % 2) * bit
        return to // clips, to % clips

    def mask_of(k):
        crossing = 1 - k // half
        low = k % half
        swap = ((low // quarter + crossing * odd) % 2) * quarter
        return crossing * half + swap + low % quarter

    barrier = pltpu.get_barrier_semaphore()

    @pl.loop(1, count)
    def _(mask):
        pl.semaphore_signal(barrier, inc=1, device_id=other(mask), device_id_type=MESH)

    for buffer in (edge_in, face_in, corner_in, volume):
        buffer[...] = jnp.zeros_like(buffer)
    chunks = rows // LANES
    before = (iota((LANES, 2 * LANES), 0) < iota((LANES, 2 * LANES), 1)).astype(F32).astype(BF16)
    for load in loads[:2]:
        load.wait()
    owner = owner_ref[...]
    slot = slot_ref[...]
    to_clip = owner >> bits(tiles)
    mask = ((owner & (tiles - 1)) * clips + to_clip) ^ me
    crossing = mask >> (depth - 1)
    order = mask ^ half ^ (crossing * (odd * quarter))
    table = (iota((count, rows), 0) == order).astype(F32)
    table16 = table.astype(BF16)
    stacked = jnp.concatenate([table16[:, c * LANES : (c + 1) * LANES] for c in range(chunks)], axis=0)
    counted = dot(stacked, before)
    base = jnp.zeros((count, LANES), F32)
    ranks = []
    for c in range(chunks):
        part = counted[c * count : (c + 1) * count]
        hit = table[:, c * LANES : (c + 1) * LANES]
        ranks.append(jnp.sum((part[:, :LANES] + base) * hit, axis=0, keepdims=True))
        base = base + part[:, LANES:]
    rank = jnp.concatenate(ranks, axis=1).astype(jnp.int32)
    position = order * cap + rank

    label = slot + 1
    by_rank = (iota((LANES, rows), 0) == rank).astype(F32).astype(BF16)
    digits = jnp.concatenate(
        [table * (label >> 5).astype(F32), table * (label & 31).astype(F32)], axis=0
    ).astype(BF16)
    labels = lax.dot_general(digits, by_rank, NT, preferred_element_type=F32)
    labels = labels[:count] * 32.0 + labels[count:]

    for load in loads[2:4]:
        load.wait()
    for load in weight_loads:
        load.start()
    values = rows_ref[...]
    per_group = bits(channels // GROUPS)

    def partial_sums():
        clip_row = iota((8, rows), 0)
        live_limit = jnp.zeros((8, rows), jnp.int32)
        for c in range(clips):
            live_limit = jnp.where(clip_row == c, live_ref[c] * PLANE, live_limit)
        live_row = ((clip_row == to_clip) & (slot < live_limit)).astype(F32).astype(BF16)
        wide = values.astype(F32)
        square = wide * wide
        high = square.astype(BF16)
        low = (square - high.astype(F32)).astype(BF16)
        sum1 = dot(live_row, values)
        sum2 = dot(live_row, high) + dot(live_row, low)
        group = iota((channels, LANES), 0) >> per_group
        lane = iota((channels, LANES), 1)
        partial = dot(sum1, (lane - STAT == group).astype(F32), precision=HIGHEST) + dot(
            sum2, (lane - STAT - GROUPS == group).astype(F32), precision=HIGHEST
        )
        goes = (my_clip ^ iota((count, LANES), 0)) & (clips - 1)
        stats = jnp.zeros((count, LANES), F32)
        for c in range(clips):
            stats = jnp.where(goes == c, partial[c : c + 1], stats)
        return stats

    def row_copy(k):
        mask = mask_of(k)
        return pltpu.make_async_remote_copy(
            src_ref=send_rows.at[k],
            dst_ref=recv_rows.at[mask],
            send_sem=row_sent.at[k],
            recv_sem=row_got.at[mask],
            device_id=other(mask),
            device_id_type=MESH,
        )

    def meta_copy(k):
        mask = mask_of(k)
        return pltpu.make_async_remote_copy(
            src_ref=send_meta.at[k],
            dst_ref=recv_meta.at[mask],
            send_sem=meta_sent.at[k],
            recv_sem=meta_got.at[mask],
            device_id=other(mask),
            device_id_type=MESH,
        )

    batch = max(1, min(quarter, 512 // cap))
    while quarter % batch:
        batch -= 1
    size = batch * cap

    def pack(first):
        chosen = (iota((size, rows), 0) + first * cap == position).astype(F32).astype(BF16)
        packed = dot(chosen, values).astype(BF16)
        send_rows[first : first + batch] = packed.reshape(batch, cap, channels)

    metas = labels + partial_sums()
    for k in range(count):
        send_meta[k] = metas[k : k + 1]
    recv_meta[0] = send_meta[own]
    pack(0)
    pl.semaphore_wait(barrier, count - 1)

    @pl.loop(0, count)
    def _(k):
        @pl.when(k != own)
        def _():
            meta_copy(k).start()

    for first in range(0, count, batch):
        if first:
            pack(first)

        @pl.loop(first, first + batch)
        def _(k):
            @pl.when(k != own)
            def _():
                row_copy(k).start()

    recv_rows[0] = send_rows[own]

    @pl.loop(0, count)
    def _(k):
        @pl.when(k != own)
        def _():
            meta_copy(k).wait_recv()

    joint = joint_of(count, cap)
    width = joint * cap
    groups = count // joint
    metas_in = jnp.concatenate([recv_meta[m] for m in range(count)], axis=0)
    spread_lane = iota((LANES, width), 0)
    spread_col = iota((LANES, width), 1)
    spread = jnp.zeros((LANES, width), F32)
    block_of = jnp.zeros((count, width), jnp.int32)
    for m in range(joint):
        spread = jnp.where((spread_col - m * cap == spread_lane) & (spread_lane < cap), 1.0, spread)
        block_of = jnp.where(iota((count, width), 1) >= m * cap, m, block_of)
    moved = dot(metas_in, spread, precision=HIGHEST)
    source_of = iota((count, width), 0)
    for q in range(groups):
        keep = source_of == block_of + q * joint
        row = jnp.sum(jnp.where(keep, moved, 0.0), axis=0, keepdims=True)
        slots_ref[q] = (row + 0.5).astype(jnp.int32) - 1

    for load in loads[4:]:
        load.wait()
    live = live_ref[my_clip]
    sums_in = jnp.broadcast_to(jnp.sum(metas_in, axis=0, keepdims=True), (8, LANES))
    voxels = jnp.full((8, LANES), live * ((channels // GROUPS) * PLANE * tiles), jnp.int32)
    scaled = sums_in / voxels.astype(F32)
    stat_lane = iota((LANES, channels), 0)
    stat_group = iota((LANES, channels), 1) >> per_group
    mean = dot(scaled, (stat_lane - STAT == stat_group).astype(F32), precision=HIGHEST)
    second = dot(scaled, (stat_lane - STAT - GROUPS == stat_group).astype(F32), precision=HIGHEST)
    scale = lax.rsqrt(second - mean * mean + EPSILON)
    scale = (0.5 * (scale * gain_ref[...]))[0:1]
    mean = mean[0:1]
    bias = 0.5 * bias_ref[...]

    def activate(raw):
        u = (raw.astype(F32) - mean) * scale + bias
        return (u + u * jnp.tanh(u)).astype(BF16)

    edge_row = iota((EDGE, width), 0)
    edge_voxel = edge_row * TW + jnp.where(edge_row < EDGE // 2, TW - 1, -rows)
    voxel = jnp.concatenate([iota((rows, width), 0), edge_voxel], axis=0)

    def place(q):
        @pl.loop(0, joint)
        def _(i):
            mask = q * joint + i

            @pl.when(mask != 0)
            def _():
                pltpu.make_async_remote_copy(
                    src_ref=send_rows.at[0],
                    dst_ref=recv_rows.at[mask],
                    send_sem=row_sent.at[0],
                    recv_sem=row_got.at[mask],
                    device_id=other(mask),
                    device_id_type=MESH,
                ).wait_recv()

        target = (voxel == slots_ref[q]).astype(F32).astype(BF16)
        arrived = recv_rows[pl.ds(q * joint, joint)].reshape(width, channels)
        return dot(target, activate(arrived)).astype(BF16)

    half_groups = groups // 2
    quarter_groups = groups // 4
    flip = (odd + 1 - far) % 2

    def group_of(p):
        late = p // half_groups
        low = p % half_groups
        swap = (low // quarter_groups + late * flip) % 2
        return late * half_groups + swap * quarter_groups + low % quarter_groups

    placed_ref[...] = place(0)

    @pl.loop(1, groups - 1)
    def _(p):
        placed_ref[...] += place(group_of(p))

    tile = placed_ref[...] + place(group_of(groups - 1))
    edge_out[...] = tile[rows:]
    grid = tile[:rows].reshape(LT, TH, TW, channels)
    for a in range(3):
        volume[2 - a :, 1 : TH + 1, :, a * channels : (a + 1) * channels] = grid[: LT - 2 + a]

    grid_rows = tiles // GW
    row_tile = my_tile // GW
    column_tile = my_tile % GW

    def exists(down, right):
        row = row_tile + down
        column = column_tile + right
        return (row >= 0) & (row < grid_rows) & (column >= 0) & (column < GW)

    def halo_copy(e):
        down, right = EDGES[e]
        if e < 2:
            part, source_ref, target_ref = pl.ds(e * (EDGE // 2), EDGE // 2), edge_out, edge_in
        elif e < 4:
            part, source_ref, target_ref = e - 2, face_out, face_in
        else:
            part, source_ref, target_ref = e - 4, corner_out, corner_in
        return pltpu.make_async_remote_copy(
            src_ref=source_ref.at[part],
            dst_ref=target_ref.at[part],
            send_sem=halo_sent.at[e],
            recv_sem=halo_got.at[e],
            device_id=(my_tile + down * GW + right, my_clip),
            device_id_type=MESH,
        )

    def send(e):
        @pl.when(exists(*EDGES[e]))
        def _():
            halo_copy(e).start()

    def receive(e):
        down, right = EDGES[e]

        @pl.when(exists(-down, -right))
        def _():
            halo_copy(e).wait_recv()

    send(0)
    send(1)
    for load in weight_loads:
        load.wait()

    def shifted(product, column):
        taps = [product[:, d * out_width : (d + 1) * out_width] for d in range(3)]
        n = product.shape[0]
        after = jnp.where(column == 0, 0.0, pltpu.roll(taps[0], 1, 0))
        ahead = jnp.where(column == TW - 1, 0.0, pltpu.roll(taps[2], n - 1, 0))
        return after + taps[1] + ahead

    lines = LT * TW
    line_column = iota((lines, out_width), 0) & (TW - 1)
    for f in range(2):
        @pl.when(exists(1 - 2 * f, 0))
        def _():
            b, h = (0, TH) if f == 0 else (2, 1)
            outer = dot(volume[:, h].reshape(lines, 3 * channels), weight_ref[b])
            face_out[f] = shifted(outer, line_column).astype(BF16)
            send(2 + f)
            by_frame = outer.reshape(LT, TW, 3 * out_width)
            for g in range(2):
                w, d = (TW - 1, 0) if g == 0 else (0, 2)
                corner = by_frame[:, w, d * out_width : (d + 1) * out_width]
                corner_out[2 * f + g] = jnp.concatenate(
                    [corner[:, : out_width // 2], corner[:, out_width // 2 :]], axis=0
                )
                send(4 + 2 * f + g)

    plane_column = iota((PLANE, out_width), 0) & (TW - 1)

    def frame_sum(t, extra):
        skip = max(0, 2 - t) * channels
        product = None
        for b in range(3):
            slab = volume[t, b : b + TH, :, skip:].reshape(PLANE, 3 * channels - skip)
            if extra:
                slab = jnp.concatenate([slab, side[b]], axis=0)
            term = dot(slab, weight_ref[b, skip:])
            product = term if product is None else product + term
        summed[t] = shifted(product[:PLANE], plane_column)
        return product[PLANE:]

    for t in range(LT - 1):
        frame_sum(t, False)
    receive(0)
    receive(1)
    edges = edge_in[...]
    at = iota((9 * EDGE, EDGE), 0)
    tap = at // EDGE
    line = at % EDGE
    h = line % TH + tap // 3 - 1
    t = (line // TH) % LT + tap % 3 - 2
    from_line = (line // (EDGE // 2)) * (EDGE // 2) + t * TH + h
    inside = (h >= 0) & (h < TH) & (t >= 0)
    picked = ((iota((9 * EDGE, EDGE), 1) == from_line) & inside).astype(F32).astype(BF16)
    picked = dot(picked, edges).astype(BF16)
    for b in range(3):
        for a in range(3):
            n = b * 3 + a
            side[b, :, a * channels : (a + 1) * channels] = picked[n * EDGE : (n + 1) * EDGE]
    beside = frame_sum(LT - 1, True)
    left = beside[: EDGE // 2, :out_width]
    right = beside[EDGE // 2 :, 2 * out_width :]
    for e in range(2, 8):
        receive(e)

    column = iota((TW, out_width), 0)
    out_bias = out_bias_ref[...]

    def corner_of(i, t):
        return jnp.concatenate([corner_in[i, t : t + 1], corner_in[i, LT + t : LT + t + 1]], axis=1)

    for t in range(LT):
        for h in range(TH):
            n = t * TH + h
            first, last = left[n : n + 1], right[n : n + 1]
            total = summed[t, h * TW : (h + 1) * TW] + out_bias
            if h in (0, TH - 1):
                f = 0 if h == 0 else 1
                total = total + face_in[f, t * TW : (t + 1) * TW].astype(F32)
                first = first + corner_of(2 * f, t)
                last = last + corner_of(2 * f + 1, t)
            total = total + jnp.where(column == 0, first, 0.0) + jnp.where(column == TW - 1, last, 0.0)
            out_ref[n * TW : (n + 1) * TW] = jnp.where(t < live, total, 0.0).astype(BF16)

    @pl.loop(0, count)
    def _(k):
        @pl.when(k != own)
        def _():
            meta_copy(k).wait_send()
            row_copy(k).wait_send()

    for e, (down, right) in enumerate(EDGES):
        @pl.when(exists(down, right))
        def _():
            halo_copy(e).wait_send()


def on_device(
    seq_rows, plan_owner, plan_slot, live_frames, norm_gain, norm_bias, conv_weight, conv_bias
):
    rows, channels = seq_rows.shape
    out_width = conv_bias.shape[0]
    tiles = lax.axis_size("tile")
    clips = lax.axis_size("clip")
    count = tiles * clips
    cap = -(-(3 * (rows // count) // 2) // 16) * 16
    joint = joint_of(count, cap)
    dma = pltpu.SemaphoreType.DMA
    decoded = pl.pallas_call(
        functools.partial(decode_kernel, tiles, clips, cap),
        out_shape=jax.ShapeDtypeStruct((rows, out_width), BF16),
        in_specs=[pl.BlockSpec(memory_space=pltpu.HBM)] * 8,
        out_specs=pl.BlockSpec(memory_space=pltpu.VMEM),
        scratch_shapes=[
            pltpu.SMEM((clips,), jnp.int32),
            pltpu.VMEM((1, rows), jnp.int32),
            pltpu.VMEM((1, rows), jnp.int32),
            pltpu.VMEM((rows, channels), BF16),
            pltpu.VMEM((1, channels), F32),
            pltpu.VMEM((1, channels), F32),
            pltpu.VMEM((1, out_width), F32),
            pltpu.VMEM((3, 3 * channels, 3 * out_width), BF16),
            pltpu.VMEM((count, cap, channels), BF16),
            pltpu.VMEM((count, cap, channels), BF16),
            pltpu.VMEM((count, 1, LANES), F32),
            pltpu.VMEM((count, 1, LANES), F32),
            pltpu.VMEM((count // joint, 1, joint * cap), jnp.int32),
            pltpu.VMEM((rows + EDGE, channels), BF16),
            pltpu.VMEM((LT, TH + 2, TW, 3 * channels), BF16),
            pltpu.VMEM((3, EDGE, 3 * channels), BF16),
            pltpu.VMEM((EDGE, channels), BF16),
            pltpu.VMEM((EDGE, channels), BF16),
            pltpu.VMEM((2, LT * TW, out_width), BF16),
            pltpu.VMEM((2, LT * TW, out_width), BF16),
            pltpu.VMEM((4, 2 * LT, out_width // 2), F32),
            pltpu.VMEM((4, 2 * LT, out_width // 2), F32),
            pltpu.VMEM((LT, PLANE, out_width), F32),
            dma((7,)),
            dma((27,)),
            dma((count,)),
            dma((count,)),
            dma((count,)),
            dma((count,)),
            dma((8,)),
            dma((8,)),
        ],
        compiler_params=pltpu.CompilerParams(
            collective_id=0, has_side_effects=True, vmem_limit_bytes=56 << 20
        ),
        name="decode",
    )(
        live_frames,
        plan_owner.reshape(1, rows),
        plan_slot.reshape(1, rows),
        seq_rows,
        norm_gain.reshape(1, channels),
        norm_bias.reshape(1, channels),
        conv_bias.reshape(1, out_width),
        conv_weight.transpose(0, 1, 3, 2, 4).reshape(9, 3 * channels, out_width),
    )
    return decoded.reshape(1, 1, LT, TH, TW, out_width)


def solution(mesh):
    return jax.shard_map(
        on_device,
        mesh=mesh,
        in_specs=(
            P(("tile", "clip"), None),
            P(("tile", "clip")),
            P(("tile", "clip")),
            P(),
            P(),
            P(),
            P(),
            P(),
        ),
        out_specs=P("clip", "tile", None, None, None, None),
        check_vma=False,
    )
```

```python
import functools

import jax
import jax.numpy as jnp
from jax import lax
from jax.experimental import pallas as pl
from jax.experimental.pallas import tpu as pltpu
from jax.sharding import PartitionSpec as P

GROUPS = 32
LT = 4
TH = 8
TW = 32
GW = 4
PLANE = TH * TW
LANES = 128
STAT = 64
EDGE = 2 * LT * TH
EPSILON = 1e-06
HIGHEST = lax.Precision.HIGHEST
F32 = jnp.float32
BF16 = jnp.bfloat16
NT = (((1,), (1,)), ((), ()))
MESH = pl.DeviceIdType.MESH
EDGES = ((0, 1), (0, -1), (1, 0), (-1, 0), (1, 1), (1, -1), (-1, 1), (-1, -1))


def iota(shape, axis):
    return lax.broadcasted_iota(jnp.int32, shape, axis)


def bits(n):
    return n.bit_length() - 1


def dot(a, b, **kw):
    return jnp.dot(a, b, preferred_element_type=F32, **kw)


def joint_of(count, cap):
    joint = max(1, min(count // 4, 256 // cap))
    while (count // 4) % joint:
        joint -= 1
    return joint


def decode_kernel(
    tiles,
    clips,
    cap,
    live_hbm,
    owner_hbm,
    slot_hbm,
    rows_hbm,
    gain_hbm,
    bias_hbm,
    out_bias_hbm,
    weight_hbm,
    out_ref,
    live_ref,
    owner_ref,
    slot_ref,
    rows_ref,
    gain_ref,
    bias_ref,
    out_bias_ref,
    weight_ref,
    send_rows,
    recv_rows,
    send_meta,
    recv_meta,
    slots_ref,
    placed_ref,
    volume,
    side,
    edge_out,
    edge_in,
    face_out,
    face_in,
    corner_out,
    corner_in,
    summed,
    loaded,
    weight_loaded,
    row_sent,
    row_got,
    meta_sent,
    meta_got,
    halo_sent,
    halo_got,
):
    loads = [
        pltpu.make_async_copy(source, target, loaded.at[i])
        for i, (source, target) in enumerate(
            (
                (owner_hbm, owner_ref),
                (slot_hbm, slot_ref),
                (live_hbm, live_ref),
                (rows_hbm, rows_ref),
                (gain_hbm, gain_ref),
                (bias_hbm, bias_ref),
                (out_bias_hbm, out_bias_ref),
            )
        )
    ]
    for load in loads:
        load.start()
    rows, channels = rows_ref.shape
    out_width = out_bias_ref.shape[1]
    weight_loads = [
        pltpu.make_async_copy(
            weight_hbm.at[a * 3 + b, pl.ds(d * channels, channels)],
            weight_ref.at[b, pl.ds(a * channels, channels), pl.ds(d * out_width, out_width)],
            weight_loaded.at[(a * 3 + b) * 3 + d],
        )
        for a in range(3)
        for b in range(3)
        for d in range(3)
    ]
    count = tiles * clips
    depth = bits(count)
    half = count // 2
    quarter = count // 4
    own = half
    my_tile = lax.axis_index("tile")
    my_clip = lax.axis_index("clip")
    me = my_tile * clips + my_clip
    far = me // half
    odd = (me // quarter) % 2

    def other(mask):
        to = 0
        for i in range(depth):
            bit = 1 << i
            to = to + ((me // bit + mask // bit) % 2) * bit
        return to // clips, to % clips

    def mask_of(k):
        crossing = 1 - k // half
        low = k % half
        swap = ((low // quarter + crossing * odd) % 2) * quarter
        return crossing * half + swap + low % quarter

    barrier = pltpu.get_barrier_semaphore()

    @pl.loop(1, count)
    def _(mask):
        pl.semaphore_signal(barrier, inc=1, device_id=other(mask), device_id_type=MESH)

    for buffer in (edge_in, face_in, corner_in, volume):
        buffer[...] = jnp.zeros_like(buffer)
    chunks = rows // LANES
    before = (iota((LANES, 2 * LANES), 0) < iota((LANES, 2 * LANES), 1)).astype(F32).astype(BF16)
    for load in loads[:2]:
        load.wait()
    owner = owner_ref[...]
    slot = slot_ref[...]
    to_clip = owner >> bits(tiles)
    mask = ((owner & (tiles - 1)) * clips + to_clip) ^ me
    crossing = mask >> (depth - 1)
    order = mask ^ half ^ (crossing * (odd * quarter))
    table = (iota((count, rows), 0) == order).astype(F32)
    table16 = table.astype(BF16)
    stacked = jnp.concatenate([table16[:, c * LANES : (c + 1) * LANES] for c in range(chunks)], axis=0)
    counted = dot(stacked, before)
    base = jnp.zeros((count, LANES), F32)
    ranks = []
    for c in range(chunks):
        part = counted[c * count : (c + 1) * count]
        hit = table[:, c * LANES : (c + 1) * LANES]
        ranks.append(jnp.sum((part[:, :LANES] + base) * hit, axis=0, keepdims=True))
        base = base + part[:, LANES:]
    rank = jnp.concatenate(ranks, axis=1).astype(jnp.int32)
    position = order * cap + rank

    label = slot + 1
    by_rank = (iota((LANES, rows), 0) == rank).astype(F32).astype(BF16)
    digits = jnp.concatenate(
        [table * (label >> 5).astype(F32), table * (label & 31).astype(F32)], axis=0
    ).astype(BF16)
    labels = lax.dot_general(digits, by_rank, NT, preferred_element_type=F32)
    labels = labels[:count] * 32.0 + labels[count:]

    for load in loads[2:4]:
        load.wait()
    for load in weight_loads:
        load.start()
    values = rows_ref[...]
    per_group = bits(channels // GROUPS)

    def partial_sums():
        clip_row = iota((8, rows), 0)
        live_limit = jnp.zeros((8, rows), jnp.int32)
        for c in range(clips):
            live_limit = jnp.where(clip_row == c, live_ref[c] * PLANE, live_limit)
        live_row = ((clip_row == to_clip) & (slot < live_limit)).astype(F32).astype(BF16)
        wide = values.astype(F32)
        square = wide * wide
        high = square.astype(BF16)
        low = (square - high.astype(F32)).astype(BF16)
        sum1 = dot(live_row, values)
        sum2 = dot(live_row, high) + dot(live_row, low)
        group = iota((channels, LANES), 0) >> per_group
        lane = iota((channels, LANES), 1)
        partial = dot(sum1, (lane - STAT == group).astype(F32), precision=HIGHEST) + dot(
            sum2, (lane - STAT - GROUPS == group).astype(F32), precision=HIGHEST
        )
        goes = (my_clip ^ iota((count, LANES), 0)) & (clips - 1)
        stats = jnp.zeros((count, LANES), F32)
        for c in range(clips):
            stats = jnp.where(goes == c, partial[c : c + 1], stats)
        return stats

    def row_copy(k):
        mask = mask_of(k)
        return pltpu.make_async_remote_copy(
            src_ref=send_rows.at[k],
            dst_ref=recv_rows.at[mask],
            send_sem=row_sent.at[k],
            recv_sem=row_got.at[mask],
            device_id=other(mask),
            device_id_type=MESH,
        )

    def meta_copy(k):
        mask = mask_of(k)
        return pltpu.make_async_remote_copy(
            src_ref=send_meta.at[k],
            dst_ref=recv_meta.at[mask],
            send_sem=meta_sent.at[k],
            recv_sem=meta_got.at[mask],
            device_id=other(mask),
            device_id_type=MESH,
        )

    batch = max(1, min(quarter, 512 // cap))
    while quarter % batch:
        batch -= 1
    size = batch * cap

    def pack(first):
        chosen = (iota((size, rows), 0) + first * cap == position).astype(F32).astype(BF16)
        packed = dot(chosen, values).astype(BF16)
        send_rows[first : first + batch] = packed.reshape(batch, cap, channels)

    metas = labels + partial_sums()
    for k in range(count):
        send_meta[k] = metas[k : k + 1]
    recv_meta[0] = send_meta[own]
    pack(0)
    pl.semaphore_wait(barrier, count - 1)

    @pl.loop(0, count)
    def _(k):
        @pl.when(k != own)
        def _():
            meta_copy(k).start()

    for first in range(0, half, batch):
        if first:
            pack(first)
        pack(half + first)

        @pl.loop(first, first + batch)
        def _(k):
            row_copy(k).start()

            @pl.when(k != 0)
            def _():
                row_copy(half + k).start()

    recv_rows[0] = send_rows[own]

    @pl.loop(0, count)
    def _(k):
        @pl.when(k != own)
        def _():
            meta_copy(k).wait_recv()

    joint = joint_of(count, cap)
    width = joint * cap
    groups = count // joint
    metas_in = jnp.concatenate([recv_meta[m] for m in range(count)], axis=0)
    spread_lane = iota((LANES, width), 0)
    spread_col = iota((LANES, width), 1)
    spread = jnp.zeros((LANES, width), F32)
    block_of = jnp.zeros((count, width), jnp.int32)
    for m in range(joint):
        spread = jnp.where((spread_col - m * cap == spread_lane) & (spread_lane < cap), 1.0, spread)
        block_of = jnp.where(iota((count, width), 1) >= m * cap, m, block_of)
    moved = dot(metas_in, spread, precision=HIGHEST)
    source_of = iota((count, width), 0)
    for q in range(groups):
        keep = source_of == block_of + q * joint
        row = jnp.sum(jnp.where(keep, moved, 0.0), axis=0, keepdims=True)
        slots_ref[q] = (row + 0.5).astype(jnp.int32) - 1

    for load in loads[4:]:
        load.wait()
    live = live_ref[my_clip]
    sums_in = jnp.broadcast_to(jnp.sum(metas_in, axis=0, keepdims=True), (8, LANES))
    voxels = jnp.full((8, LANES), live * ((channels // GROUPS) * PLANE * tiles), jnp.int32)
    scaled = sums_in / voxels.astype(F32)
    stat_lane = iota((LANES, channels), 0)
    stat_group = iota((LANES, channels), 1) >> per_group
    mean = dot(scaled, (stat_lane - STAT == stat_group).astype(F32), precision=HIGHEST)
    second = dot(scaled, (stat_lane - STAT - GROUPS == stat_group).astype(F32), precision=HIGHEST)
    scale = lax.rsqrt(second - mean * mean + EPSILON)
    scale = (0.5 * (scale * gain_ref[...]))[0:1]
    mean = mean[0:1]
    bias = 0.5 * bias_ref[...]

    def activate(raw):
        u = (raw.astype(F32) - mean) * scale + bias
        return (u + u * jnp.tanh(u)).astype(BF16)

    edge_row = iota((EDGE, width), 0)
    edge_voxel = edge_row * TW + jnp.where(edge_row < EDGE // 2, TW - 1, -rows)
    voxel = jnp.concatenate([iota((rows, width), 0), edge_voxel], axis=0)

    def place(q):
        @pl.loop(0, joint)
        def _(i):
            mask = q * joint + i

            @pl.when(mask != 0)
            def _():
                pltpu.make_async_remote_copy(
                    src_ref=send_rows.at[0],
                    dst_ref=recv_rows.at[mask],
                    send_sem=row_sent.at[0],
                    recv_sem=row_got.at[mask],
                    device_id=other(mask),
                    device_id_type=MESH,
                ).wait_recv()

        target = (voxel == slots_ref[q]).astype(F32).astype(BF16)
        arrived = recv_rows[pl.ds(q * joint, joint)].reshape(width, channels)
        return dot(target, activate(arrived)).astype(BF16)

    half_groups = groups // 2
    quarter_groups = groups // 4
    flip = (odd + 1 - far) % 2

    def group_of(p):
        late = p // half_groups
        low = p % half_groups
        swap = (low // quarter_groups + late * flip) % 2
        return late * half_groups + swap * quarter_groups + low % quarter_groups

    placed_ref[...] = place(0)

    @pl.loop(1, groups - 1)
    def _(p):
        placed_ref[...] += place(group_of(p))

    tile = placed_ref[...] + place(group_of(groups - 1))
    edge_out[...] = tile[rows:]
    grid = tile[:rows].reshape(LT, TH, TW, channels)
    for a in range(3):
        volume[2 - a :, 1 : TH + 1, :, a * channels : (a + 1) * channels] = grid[: LT - 2 + a]

    grid_rows = tiles // GW
    row_tile = my_tile // GW
    column_tile = my_tile % GW

    def exists(down, right):
        row = row_tile + down
        column = column_tile + right
        return (row >= 0) & (row < grid_rows) & (column >= 0) & (column < GW)

    def halo_copy(e):
        down, right = EDGES[e]
        if e < 2:
            part, source_ref, target_ref = pl.ds(e * (EDGE // 2), EDGE // 2), edge_out, edge_in
        elif e < 4:
            part, source_ref, target_ref = e - 2, face_out, face_in
        else:
            part, source_ref, target_ref = e - 4, corner_out, corner_in
        return pltpu.make_async_remote_copy(
            src_ref=source_ref.at[part],
            dst_ref=target_ref.at[part],
            send_sem=halo_sent.at[e],
            recv_sem=halo_got.at[e],
            device_id=(my_tile + down * GW + right, my_clip),
            device_id_type=MESH,
        )

    def send(e):
        @pl.when(exists(*EDGES[e]))
        def _():
            halo_copy(e).start()

    def receive(e):
        down, right = EDGES[e]

        @pl.when(exists(-down, -right))
        def _():
            halo_copy(e).wait_recv()

    send(0)
    send(1)
    for load in weight_loads:
        load.wait()

    def shifted(product, column):
        taps = [product[:, d * out_width : (d + 1) * out_width] for d in range(3)]
        n = product.shape[0]
        after = jnp.where(column == 0, 0.0, pltpu.roll(taps[0], 1, 0))
        ahead = jnp.where(column == TW - 1, 0.0, pltpu.roll(taps[2], n - 1, 0))
        return after + taps[1] + ahead

    lines = LT * TW
    line_column = iota((lines, out_width), 0) & (TW - 1)
    for f in range(2):
        @pl.when(exists(1 - 2 * f, 0))
        def _():
            b, h = (0, TH) if f == 0 else (2, 1)
            outer = dot(volume[:, h].reshape(lines, 3 * channels), weight_ref[b])
            face_out[f] = shifted(outer, line_column).astype(BF16)
            send(2 + f)
            by_frame = outer.reshape(LT, TW, 3 * out_width)
            for g in range(2):
                w, d = (TW - 1, 0) if g == 0 else (0, 2)
                corner = by_frame[:, w, d * out_width : (d + 1) * out_width]
                corner_out[2 * f + g] = jnp.concatenate(
                    [corner[:, : out_width // 2], corner[:, out_width // 2 :]], axis=0
                )
                send(4 + 2 * f + g)

    plane_column = iota((PLANE, out_width), 0) & (TW - 1)

    def frame_sum(t, extra):
        skip = max(0, 2 - t) * channels
        product = None
        for b in range(3):
            slab = volume[t, b : b + TH, :, skip:].reshape(PLANE, 3 * channels - skip)
            if extra:
                slab = jnp.concatenate([slab, side[b]], axis=0)
            term = dot(slab, weight_ref[b, skip:])
            product = term if product is None else product + term
        summed[t] = shifted(product[:PLANE], plane_column)
        return product[PLANE:]

    for t in range(LT - 1):
        frame_sum(t, False)
    receive(0)
    receive(1)
    edges = edge_in[...]
    at = iota((9 * EDGE, EDGE), 0)
    tap = at // EDGE
    line = at % EDGE
    h = line % TH + tap // 3 - 1
    t = (line // TH) % LT + tap % 3 - 2
    from_line = (line // (EDGE // 2)) * (EDGE // 2) + t * TH + h
    inside = (h >= 0) & (h < TH) & (t >= 0)
    picked = ((iota((9 * EDGE, EDGE), 1) == from_line) & inside).astype(F32).astype(BF16)
    picked = dot(picked, edges).astype(BF16)
    for b in range(3):
        for a in range(3):
            n = b * 3 + a
            side[b, :, a * channels : (a + 1) * channels] = picked[n * EDGE : (n + 1) * EDGE]
    beside = frame_sum(LT - 1, True)
    left = beside[: EDGE // 2, :out_width]
    right = beside[EDGE // 2 :, 2 * out_width :]
    for e in range(2, 8):
        receive(e)

    column = iota((TW, out_width), 0)
    out_bias = out_bias_ref[...]

    def corner_of(i, t):
        return jnp.concatenate([corner_in[i, t : t + 1], corner_in[i, LT + t : LT + t + 1]], axis=1)

    for t in range(LT):
        for h in range(TH):
            n = t * TH + h
            first, last = left[n : n + 1], right[n : n + 1]
            total = summed[t, h * TW : (h + 1) * TW] + out_bias
            if h in (0, TH - 1):
                f = 0 if h == 0 else 1
                total = total + face_in[f, t * TW : (t + 1) * TW].astype(F32)
                first = first + corner_of(2 * f, t)
                last = last + corner_of(2 * f + 1, t)
            total = total + jnp.where(column == 0, first, 0.0) + jnp.where(column == TW - 1, last, 0.0)
            out_ref[n * TW : (n + 1) * TW] = jnp.where(t < live, total, 0.0).astype(BF16)

    @pl.loop(0, count)
    def _(k):
        @pl.when(k != own)
        def _():
            meta_copy(k).wait_send()
            row_copy(k).wait_send()

    for e, (down, right) in enumerate(EDGES):
        @pl.when(exists(down, right))
        def _():
            halo_copy(e).wait_send()


def on_device(
    seq_rows, plan_owner, plan_slot, live_frames, norm_gain, norm_bias, conv_weight, conv_bias
):
    rows, channels = seq_rows.shape
    out_width = conv_bias.shape[0]
    tiles = lax.axis_size("tile")
    clips = lax.axis_size("clip")
    count = tiles * clips
    cap = -(-(3 * (rows // count) // 2) // 16) * 16
    joint = joint_of(count, cap)
    dma = pltpu.SemaphoreType.DMA
    decoded = pl.pallas_call(
        functools.partial(decode_kernel, tiles, clips, cap),
        out_shape=pltpu.VMEM((rows, out_width), BF16),
        in_specs=[pl.BlockSpec(memory_space=pltpu.HBM)] * 8,
        out_specs=pl.BlockSpec(memory_space=pltpu.VMEM),
        scratch_shapes=[
            pltpu.SMEM((clips,), jnp.int32),
            pltpu.VMEM((1, rows), jnp.int32),
            pltpu.VMEM((1, rows), jnp.int32),
            pltpu.VMEM((rows, channels), BF16),
            pltpu.VMEM((1, channels), F32),
            pltpu.VMEM((1, channels), F32),
            pltpu.VMEM((1, out_width), F32),
            pltpu.VMEM((3, 3 * channels, 3 * out_width), BF16),
            pltpu.VMEM((count, cap, channels), BF16),
            pltpu.VMEM((count, cap, channels), BF16),
            pltpu.VMEM((count, 1, LANES), F32),
            pltpu.VMEM((count, 1, LANES), F32),
            pltpu.VMEM((count // joint, 1, joint * cap), jnp.int32),
            pltpu.VMEM((rows + EDGE, channels), BF16),
            pltpu.VMEM((LT, TH + 2, TW, 3 * channels), BF16),
            pltpu.VMEM((3, EDGE, 3 * channels), BF16),
            pltpu.VMEM((EDGE, channels), BF16),
            pltpu.VMEM((EDGE, channels), BF16),
            pltpu.VMEM((2, LT * TW, out_width), BF16),
            pltpu.VMEM((2, LT * TW, out_width), BF16),
            pltpu.VMEM((4, 2 * LT, out_width // 2), F32),
            pltpu.VMEM((4, 2 * LT, out_width // 2), F32),
            pltpu.VMEM((LT, PLANE, out_width), F32),
            dma((7,)),
            dma((27,)),
            dma((count,)),
            dma((count,)),
            dma((count,)),
            dma((count,)),
            dma((8,)),
            dma((8,)),
        ],
        compiler_params=pltpu.CompilerParams(
            collective_id=0, has_side_effects=True, vmem_limit_bytes=56 << 20
        ),
        name="decode",
    )(
        live_frames,
        plan_owner.reshape(1, rows),
        plan_slot.reshape(1, rows),
        seq_rows,
        norm_gain.reshape(1, channels),
        norm_bias.reshape(1, channels),
        conv_bias.reshape(1, out_width),
        conv_weight.transpose(0, 1, 3, 2, 4).reshape(9, 3 * channels, out_width),
    )

    def finish(held_ref, result_ref, done):
        copy = pltpu.make_async_copy(held_ref, result_ref, done)
        copy.start()
        copy.wait()

    decoded = pl.pallas_call(
        finish,
        out_shape=jax.ShapeDtypeStruct((rows, out_width), BF16),
        in_specs=[pl.BlockSpec(memory_space=pltpu.VMEM)],
        out_specs=pl.BlockSpec(memory_space=pltpu.HBM),
        scratch_shapes=[dma],
        name="finish",
    )(pltpu.with_memory_space_constraint(decoded, pltpu.VMEM))
    return decoded.reshape(1, 1, LT, TH, TW, out_width)


def solution(mesh):
    return jax.shard_map(
        on_device,
        mesh=mesh,
        in_specs=(
            P(("tile", "clip"), None),
            P(("tile", "clip")),
            P(("tile", "clip")),
            P(),
            P(),
            P(),
            P(),
            P(),
        ),
        out_specs=P("clip", "tile", None, None, None, None),
        check_vma=False,
    )
```

```python
import functools

import jax
import jax.numpy as jnp
from jax import lax
from jax.experimental import pallas as pl
from jax.experimental.pallas import tpu as pltpu
from jax.sharding import PartitionSpec as P

GROUPS = 32
LT = 4
TH = 8
TW = 32
GW = 4
PLANE = TH * TW
LANES = 128
STAT = 64
EDGE = 2 * LT * TH
EPSILON = 1e-06
HIGHEST = lax.Precision.HIGHEST
F32 = jnp.float32
BF16 = jnp.bfloat16
NT = (((1,), (1,)), ((), ()))
MESH = pl.DeviceIdType.MESH
EDGES = ((0, 1), (0, -1), (1, 0), (-1, 0), (1, 1), (1, -1), (-1, 1), (-1, -1))


def iota(shape, axis):
    return lax.broadcasted_iota(jnp.int32, shape, axis)


def bits(n):
    return n.bit_length() - 1


def dot(a, b, **kw):
    return jnp.dot(a, b, preferred_element_type=F32, **kw)


def joint_of(count, cap):
    joint = max(1, min(count // 4, 256 // cap))
    while (count // 4) % joint:
        joint -= 1
    return joint


def decode_kernel(
    tiles,
    clips,
    cap,
    live_hbm,
    owner_hbm,
    slot_hbm,
    rows_hbm,
    gain_hbm,
    bias_hbm,
    out_bias_hbm,
    weight_hbm,
    out_ref,
    live_ref,
    owner_ref,
    slot_ref,
    rows_ref,
    gain_ref,
    bias_ref,
    out_bias_ref,
    weight_ref,
    send_rows,
    recv_rows,
    send_meta,
    recv_meta,
    slots_ref,
    placed_ref,
    volume,
    side,
    pick_ref,
    edge_out,
    edge_in,
    face_out,
    face_in,
    corner_out,
    corner_in,
    summed,
    loaded,
    weight_loaded,
    row_sent,
    row_got,
    meta_sent,
    meta_got,
    halo_sent,
    halo_got,
):
    loads = [
        pltpu.make_async_copy(source, target, loaded.at[i])
        for i, (source, target) in enumerate(
            (
                (owner_hbm, owner_ref),
                (slot_hbm, slot_ref),
                (live_hbm, live_ref),
                (rows_hbm, rows_ref),
                (gain_hbm, gain_ref),
                (bias_hbm, bias_ref),
                (out_bias_hbm, out_bias_ref),
            )
        )
    ]
    for load in loads:
        load.start()
    rows, channels = rows_ref.shape
    out_width = out_bias_ref.shape[1]
    weight_loads = [
        pltpu.make_async_copy(
            weight_hbm.at[a * 3 + b, pl.ds(d * channels, channels)],
            weight_ref.at[b, pl.ds(a * channels, channels), pl.ds(d * out_width, out_width)],
            weight_loaded.at[(a * 3 + b) * 3 + d],
        )
        for a in range(3)
        for b in range(3)
        for d in range(3)
    ]
    count = tiles * clips
    depth = bits(count)
    half = count // 2
    quarter = count // 4
    own = half
    my_tile = lax.axis_index("tile")
    my_clip = lax.axis_index("clip")
    me = my_tile * clips + my_clip
    far = me // half
    odd = (me // quarter) % 2

    signs = [1 - 2 * ((me // (1 << i)) % 2) for i in range(depth)]
    low_bits = bits(clips)

    def other(mask):
        tile, clip = my_tile, my_clip
        for i in range(depth):
            bit = (mask // (1 << i)) % 2
            if isinstance(bit, int) and not bit:
                continue
            if i < low_bits:
                clip = clip + bit * signs[i] * (1 << i)
            else:
                tile = tile + bit * signs[i] * (1 << (i - low_bits))
        return tile, clip

    def mask_of(k):
        crossing = 1 - k // half
        low = k % half
        if isinstance(k, int):
            bit = low // quarter
            swap = bit + (1 - 2 * bit) * crossing * odd
        else:
            swap = (low // quarter + crossing * odd) % 2
        return crossing * half + low % quarter, swap * quarter

    def partner(k):
        mask, extra = mask_of(k)
        tile, clip = other(mask)
        i = depth - 2
        tile = tile + (extra // quarter) * signs[i] * (1 << (i - low_bits))
        return mask + extra, (tile, clip)

    def each(begin, end, step):
        if end - begin <= 32:
            for k in range(begin, end):
                step(k)
        else:
            pl.loop(begin, end)(step)

    def unless(condition, step):
        if isinstance(condition, bool):
            if not condition:
                step()
        else:
            pl.when(jnp.logical_not(condition))(step)

    barrier = pltpu.get_barrier_semaphore()

    def announce(mask):
        pl.semaphore_signal(barrier, inc=1, device_id=other(mask), device_id_type=MESH)

    each(1, count, announce)

    for buffer in (edge_in, face_in, corner_in, volume):
        buffer[...] = jnp.zeros_like(buffer)
    chunks = rows // LANES
    before = (iota((LANES, 2 * LANES), 0) < iota((LANES, 2 * LANES), 1)).astype(F32).astype(BF16)
    for load in loads[:2]:
        load.wait()
    owner = owner_ref[...]
    slot = slot_ref[...]
    to_clip = owner >> bits(tiles)
    mask = ((owner & (tiles - 1)) * clips + to_clip) ^ me
    crossing = mask >> (depth - 1)
    order = mask ^ half ^ (crossing * (odd * quarter))
    table = (iota((count, rows), 0) == order).astype(F32)
    table16 = table.astype(BF16)
    stacked = jnp.concatenate([table16[:, c * LANES : (c + 1) * LANES] for c in range(chunks)], axis=0)
    counted = dot(stacked, before)
    base = jnp.zeros((count, LANES), F32)
    ranks = []
    for c in range(chunks):
        part = counted[c * count : (c + 1) * count]
        hit = table[:, c * LANES : (c + 1) * LANES]
        ranks.append(jnp.sum((part[:, :LANES] + base) * hit, axis=0, keepdims=True))
        base = base + part[:, LANES:]
    rank = jnp.concatenate(ranks, axis=1).astype(jnp.int32)
    position = order * cap + rank

    label = slot + 1
    by_rank = (iota((LANES, rows), 0) == rank).astype(F32).astype(BF16)
    digits = jnp.concatenate(
        [table * (label >> 5).astype(F32), table * (label & 31).astype(F32)], axis=0
    ).astype(BF16)
    labels = lax.dot_general(digits, by_rank, NT, preferred_element_type=F32)
    labels = labels[:count] * 32.0 + labels[count:]

    for load in loads[2:4]:
        load.wait()
    for load in weight_loads:
        load.start()
    values = rows_ref[...]
    per_group = bits(channels // GROUPS)

    def partial_sums():
        clip_row = iota((8, rows), 0)
        live_limit = jnp.zeros((8, rows), jnp.int32)
        for c in range(clips):
            live_limit = jnp.where(clip_row == c, live_ref[c] * PLANE, live_limit)
        live_row = ((clip_row == to_clip) & (slot < live_limit)).astype(F32).astype(BF16)
        wide = values.astype(F32)
        square = wide * wide
        high = square.astype(BF16)
        low = (square - high.astype(F32)).astype(BF16)
        sum1 = dot(live_row, values)
        sum2 = dot(live_row, high) + dot(live_row, low)
        group = iota((channels, LANES), 0) >> per_group
        lane = iota((channels, LANES), 1)
        partial = dot(sum1, (lane - STAT == group).astype(F32), precision=HIGHEST) + dot(
            sum2, (lane - STAT - GROUPS == group).astype(F32), precision=HIGHEST
        )
        goes = (my_clip ^ iota((count, LANES), 0)) & (clips - 1)
        stats = jnp.zeros((count, LANES), F32)
        for c in range(clips):
            stats = jnp.where(goes == c, partial[c : c + 1], stats)
        return stats

    def row_copy(k):
        mask, device = partner(k)
        return pltpu.make_async_remote_copy(
            src_ref=send_rows.at[k],
            dst_ref=recv_rows.at[mask],
            send_sem=row_sent.at[k],
            recv_sem=row_got.at[mask],
            device_id=device,
            device_id_type=MESH,
        )

    def meta_copy(k):
        mask, device = partner(k)
        return pltpu.make_async_remote_copy(
            src_ref=send_meta.at[k],
            dst_ref=recv_meta.at[mask],
            send_sem=meta_sent.at[k],
            recv_sem=meta_got.at[mask],
            device_id=device,
            device_id_type=MESH,
        )

    batch = max(1, min(quarter // 2, 256 // cap))
    while quarter % batch:
        batch -= 1

    def pack(first, size):
        chosen = (iota((size * cap, rows), 0) + first * cap == position).astype(F32).astype(BF16)
        packed = dot(chosen, values).astype(BF16)
        send_rows[first : first + size] = packed.reshape(size, cap, channels)

    def start_rows(begin, end):
        def step(k):
            row_copy(k).start()
            unless(k == 0, lambda: row_copy(half + k).start())

        each(begin, end, step)

    pack(0, batch)
    pack(half, batch)
    pl.semaphore_wait(barrier, count - 1)
    start_rows(0, batch)
    metas = labels + partial_sums()
    for k in range(count):
        send_meta[k] = metas[k : k + 1]
    recv_meta[0] = send_meta[own]
    each(0, count, lambda k: unless(k == own, lambda: meta_copy(k).start()))
    for first, last in ((batch, quarter), (quarter, half)):
        pack(first, last - first)
        pack(half + first, last - first)
        start_rows(first, last)
    recv_rows[0] = send_rows[own]
    each(0, count, lambda k: unless(k == own, lambda: meta_copy(k).wait_recv()))

    joint = joint_of(count, cap)
    width = joint * cap
    groups = count // joint
    metas_in = jnp.concatenate([recv_meta[m] for m in range(count)], axis=0)
    spread_lane = iota((LANES, width), 0)
    spread_col = iota((LANES, width), 1)
    spread = jnp.zeros((LANES, width), F32)
    block_of = jnp.zeros((count, width), jnp.int32)
    for m in range(joint):
        spread = jnp.where((spread_col - m * cap == spread_lane) & (spread_lane < cap), 1.0, spread)
        block_of = jnp.where(iota((count, width), 1) >= m * cap, m, block_of)
    moved = dot(metas_in, spread, precision=HIGHEST)
    source_of = iota((count, width), 0)
    for q in range(groups):
        keep = source_of == block_of + q * joint
        row = jnp.sum(jnp.where(keep, moved, 0.0), axis=0, keepdims=True)
        slots_ref[q] = (row + 0.5).astype(jnp.int32) - 1

    for load in loads[4:]:
        load.wait()
    live = live_ref[my_clip]
    sums_in = jnp.broadcast_to(jnp.sum(metas_in, axis=0, keepdims=True), (8, LANES))
    voxels = jnp.full((8, LANES), live * ((channels // GROUPS) * PLANE * tiles), jnp.int32)
    scaled = sums_in / voxels.astype(F32)
    stat_lane = iota((LANES, channels), 0)
    stat_group = iota((LANES, channels), 1) >> per_group
    mean = dot(scaled, (stat_lane - STAT == stat_group).astype(F32), precision=HIGHEST)
    second = dot(scaled, (stat_lane - STAT - GROUPS == stat_group).astype(F32), precision=HIGHEST)
    scale = lax.rsqrt(second - mean * mean + EPSILON)
    scale = (0.5 * (scale * gain_ref[...]))[0:1]
    mean = mean[0:1]
    bias = 0.5 * bias_ref[...]

    def activate(raw):
        u = (raw.astype(F32) - mean) * scale + bias
        return (u + u * jnp.tanh(u)).astype(BF16)

    edge_row = iota((EDGE, width), 0)
    edge_voxel = edge_row * TW + jnp.where(edge_row < EDGE // 2, TW - 1, -rows)
    voxel = jnp.concatenate([iota((rows, width), 0), edge_voxel], axis=0)

    def place(q):
        @pl.loop(0, joint)
        def _(i):
            mask = q * joint + i

            @pl.when(mask != 0)
            def _():
                pltpu.make_async_remote_copy(
                    src_ref=send_rows.at[0],
                    dst_ref=recv_rows.at[mask],
                    send_sem=row_sent.at[0],
                    recv_sem=row_got.at[mask],
                    device_id=other(1),
                    device_id_type=MESH,
                ).wait_recv()

        target = (voxel == slots_ref[q]).astype(F32).astype(BF16)
        arrived = recv_rows[pl.ds(q * joint, joint)].reshape(width, channels)
        return dot(target, activate(arrived)).astype(BF16)

    half_groups = groups // 2
    quarter_groups = groups // 4
    flip = (odd + 1 - far) % 2

    def group_of(p):
        late = p // half_groups
        low = p % half_groups
        swap = (low // quarter_groups + late * flip) % 2
        return late * half_groups + swap * quarter_groups + low % quarter_groups

    at = iota((9 * EDGE, EDGE), 0)
    tap = at >> bits(EDGE)
    line = at & (EDGE - 1)
    b_tap = ((tap >= 3).astype(jnp.int32) + (tap >= 6).astype(jnp.int32))
    h = (line & (TH - 1)) + b_tap - 1
    t = ((line >> bits(TH)) & (LT - 1)) + (tap - 3 * b_tap) - 2
    from_line = (line & (EDGE // 2)) + t * TH + h
    inside = (h >= 0) & (h < TH) & (t >= 0)
    pick_ref[...] = ((iota((9 * EDGE, EDGE), 1) == from_line) & inside).astype(F32).astype(BF16)
    placed_ref[...] = place(0)

    @pl.loop(1, groups - 1)
    def _(p):
        placed_ref[...] += place(group_of(p))

    tile = placed_ref[...] + place(group_of(groups - 1))
    edge_out[...] = tile[rows:]
    grid = tile[:rows].reshape(LT, TH, TW, channels)
    for a in range(3):
        volume[2 - a :, 1 : TH + 1, :, a * channels : (a + 1) * channels] = grid[: LT - 2 + a]

    grid_rows = tiles // GW
    row_tile = my_tile // GW
    column_tile = my_tile % GW

    def exists(down, right):
        row = row_tile + down
        column = column_tile + right
        return (row >= 0) & (row < grid_rows) & (column >= 0) & (column < GW)

    def halo_copy(e):
        down, right = EDGES[e]
        if e < 2:
            part, source_ref, target_ref = pl.ds(e * (EDGE // 2), EDGE // 2), edge_out, edge_in
        elif e < 4:
            part, source_ref, target_ref = e - 2, face_out, face_in
        else:
            part, source_ref, target_ref = e - 4, corner_out, corner_in
        return pltpu.make_async_remote_copy(
            src_ref=source_ref.at[part],
            dst_ref=target_ref.at[part],
            send_sem=halo_sent.at[e],
            recv_sem=halo_got.at[e],
            device_id=(my_tile + down * GW + right, my_clip),
            device_id_type=MESH,
        )

    def send(e):
        @pl.when(exists(*EDGES[e]))
        def _():
            halo_copy(e).start()

    def receive(e):
        down, right = EDGES[e]

        @pl.when(exists(-down, -right))
        def _():
            halo_copy(e).wait_recv()

    send(0)
    send(1)
    for load in weight_loads:
        load.wait()

    def shifted(product, column):
        taps = [product[:, d * out_width : (d + 1) * out_width] for d in range(3)]
        n = product.shape[0]
        after = jnp.where(column == 0, 0.0, pltpu.roll(taps[0], 1, 0))
        ahead = jnp.where(column == TW - 1, 0.0, pltpu.roll(taps[2], n - 1, 0))
        return after + taps[1] + ahead

    lines = LT * TW
    line_column = iota((lines, out_width), 0) & (TW - 1)
    for f in range(2):
        @pl.when(exists(1 - 2 * f, 0))
        def _():
            b, h = (0, TH) if f == 0 else (2, 1)
            outer = dot(volume[:, h].reshape(lines, 3 * channels), weight_ref[b])
            face_out[f] = shifted(outer, line_column).astype(BF16)
            send(2 + f)
            by_frame = outer.reshape(LT, TW, 3 * out_width)
            for g in range(2):
                w, d = (TW - 1, 0) if g == 0 else (0, 2)
                corner = by_frame[:, w, d * out_width : (d + 1) * out_width]
                corner_out[2 * f + g] = jnp.concatenate(
                    [corner[:, : out_width // 2], corner[:, out_width // 2 :]], axis=0
                )
                send(4 + 2 * f + g)

    plane_column = iota((PLANE, out_width), 0) & (TW - 1)

    def frame_sum(t, extra):
        skip = max(0, 2 - t) * channels
        product = None
        for b in range(3):
            slab = volume[t, b : b + TH, :, skip:].reshape(PLANE, 3 * channels - skip)
            if extra:
                slab = jnp.concatenate([slab, side[b]], axis=0)
            term = dot(slab, weight_ref[b, skip:])
            product = term if product is None else product + term
        summed[t] = shifted(product[:PLANE], plane_column)
        return product[PLANE:]

    for t in range(LT - 1):
        frame_sum(t, False)
    receive(0)
    receive(1)
    edges = edge_in[...]
    picked = dot(pick_ref[...], edges).astype(BF16)
    for b in range(3):
        for a in range(3):
            n = b * 3 + a
            side[b, :, a * channels : (a + 1) * channels] = picked[n * EDGE : (n + 1) * EDGE]
    beside = frame_sum(LT - 1, True)
    left = beside[: EDGE // 2, :out_width]
    right = beside[EDGE // 2 :, 2 * out_width :]
    for e in range(2, 8):
        receive(e)

    column = iota((TW, out_width), 0)
    out_bias = out_bias_ref[...]

    def corner_of(i, t):
        return jnp.concatenate([corner_in[i, t : t + 1], corner_in[i, LT + t : LT + t + 1]], axis=1)

    for t in range(LT):
        for h in range(TH):
            n = t * TH + h
            first, last = left[n : n + 1], right[n : n + 1]
            total = summed[t, h * TW : (h + 1) * TW] + out_bias
            if h in (0, TH - 1):
                f = 0 if h == 0 else 1
                total = total + face_in[f, t * TW : (t + 1) * TW].astype(F32)
                first = first + corner_of(2 * f, t)
                last = last + corner_of(2 * f + 1, t)
            total = total + jnp.where(column == 0, first, 0.0) + jnp.where(column == TW - 1, last, 0.0)
            out_ref[n * TW : (n + 1) * TW] = jnp.where(t < live, total, 0.0).astype(BF16)

    def drain(k):
        meta_copy(k).wait_send()
        row_copy(k).wait_send()

    each(0, count, lambda k: unless(k == own, lambda: drain(k)))

    for e, (down, right) in enumerate(EDGES):
        @pl.when(exists(down, right))
        def _():
            halo_copy(e).wait_send()


def on_device(
    seq_rows, plan_owner, plan_slot, live_frames, norm_gain, norm_bias, conv_weight, conv_bias
):
    rows, channels = seq_rows.shape
    out_width = conv_bias.shape[0]
    tiles = lax.axis_size("tile")
    clips = lax.axis_size("clip")
    count = tiles * clips
    cap = -(-(3 * (rows // count) // 2) // 16) * 16
    joint = joint_of(count, cap)
    dma = pltpu.SemaphoreType.DMA
    decoded = pl.pallas_call(
        functools.partial(decode_kernel, tiles, clips, cap),
        out_shape=pltpu.VMEM((rows, out_width), BF16),
        in_specs=[pl.BlockSpec(memory_space=pltpu.HBM)] * 8,
        out_specs=pl.BlockSpec(memory_space=pltpu.VMEM),
        scratch_shapes=[
            pltpu.SMEM((clips,), jnp.int32),
            pltpu.VMEM((1, rows), jnp.int32),
            pltpu.VMEM((1, rows), jnp.int32),
            pltpu.VMEM((rows, channels), BF16),
            pltpu.VMEM((1, channels), F32),
            pltpu.VMEM((1, channels), F32),
            pltpu.VMEM((1, out_width), F32),
            pltpu.VMEM((3, 3 * channels, 3 * out_width), BF16),
            pltpu.VMEM((count, cap, channels), BF16),
            pltpu.VMEM((count, cap, channels), BF16),
            pltpu.VMEM((count, 1, LANES), F32),
            pltpu.VMEM((count, 1, LANES), F32),
            pltpu.VMEM((count // joint, 1, joint * cap), jnp.int32),
            pltpu.VMEM((rows + EDGE, channels), BF16),
            pltpu.VMEM((LT, TH + 2, TW, 3 * channels), BF16),
            pltpu.VMEM((3, EDGE, 3 * channels), BF16),
            pltpu.VMEM((9 * EDGE, EDGE), BF16),
            pltpu.VMEM((EDGE, channels), BF16),
            pltpu.VMEM((EDGE, channels), BF16),
            pltpu.VMEM((2, LT * TW, out_width), BF16),
            pltpu.VMEM((2, LT * TW, out_width), BF16),
            pltpu.VMEM((4, 2 * LT, out_width // 2), F32),
            pltpu.VMEM((4, 2 * LT, out_width // 2), F32),
            pltpu.VMEM((LT, PLANE, out_width), F32),
            dma((7,)),
            dma((27,)),
            dma((count,)),
            dma((count,)),
            dma((count,)),
            dma((count,)),
            dma((8,)),
            dma((8,)),
        ],
        compiler_params=pltpu.CompilerParams(
            collective_id=0, has_side_effects=True, vmem_limit_bytes=56 << 20
        ),
        name="decode",
    )(
        live_frames,
        plan_owner.reshape(1, rows),
        plan_slot.reshape(1, rows),
        seq_rows,
        norm_gain.reshape(1, channels),
        norm_bias.reshape(1, channels),
        conv_bias.reshape(1, out_width),
        conv_weight.transpose(0, 1, 3, 2, 4).reshape(9, 3 * channels, out_width),
    )

    def finish(held_ref, result_ref, done):
        copy = pltpu.make_async_copy(held_ref, result_ref, done)
        copy.start()
        copy.wait()

    decoded = pl.pallas_call(
        finish,
        out_shape=jax.ShapeDtypeStruct((rows, out_width), BF16),
        in_specs=[pl.BlockSpec(memory_space=pltpu.VMEM)],
        out_specs=pl.BlockSpec(memory_space=pltpu.HBM),
        scratch_shapes=[dma],
        name="finish",
    )(pltpu.with_memory_space_constraint(decoded, pltpu.VMEM))
    return decoded.reshape(1, 1, LT, TH, TW, out_width)


def solution(mesh):
    return jax.shard_map(
        on_device,
        mesh=mesh,
        in_specs=(
            P(("tile", "clip"), None),
            P(("tile", "clip")),
            P(("tile", "clip")),
            P(),
            P(),
            P(),
            P(),
            P(),
        ),
        out_specs=P("clip", "tile", None, None, None, None),
        check_vma=False,
    )
```

```python
import functools

import jax
import jax.numpy as jnp
from jax import lax
from jax.experimental import pallas as pl
from jax.experimental.pallas import tpu as pltpu
from jax.sharding import PartitionSpec as P

GROUPS = 32
LT = 4
TH = 8
TW = 32
GW = 4
PLANE = TH * TW
LANES = 128
STAT = 64
EDGE = 2 * LT * TH
EPSILON = 1e-06
HIGHEST = lax.Precision.HIGHEST
F32 = jnp.float32
BF16 = jnp.bfloat16
NT = (((1,), (1,)), ((), ()))
MESH = pl.DeviceIdType.MESH
EDGES = ((0, 1), (0, -1), (1, 0), (-1, 0), (1, 1), (1, -1), (-1, 1), (-1, -1))


def iota(shape, axis):
    return lax.broadcasted_iota(jnp.int32, shape, axis)


def bits(n):
    return n.bit_length() - 1


def dot(a, b, **kw):
    return jnp.dot(a, b, preferred_element_type=F32, **kw)


def joint_of(count, cap):
    joint = max(1, min(count // 4, 256 // cap))
    while (count // 4) % joint:
        joint -= 1
    return joint


def decode_kernel(
    tiles,
    clips,
    cap,
    live_hbm,
    owner_hbm,
    slot_hbm,
    rows_hbm,
    gain_hbm,
    bias_hbm,
    out_bias_hbm,
    weight_hbm,
    out_ref,
    live_ref,
    owner_ref,
    slot_ref,
    rows_ref,
    gain_ref,
    bias_ref,
    out_bias_ref,
    weight_ref,
    send_rows,
    recv_rows,
    send_meta,
    recv_meta,
    slots_ref,
    placed_ref,
    volume,
    side,
    edge_out,
    edge_in,
    face_out,
    face_in,
    corner_out,
    corner_in,
    summed,
    loaded,
    weight_loaded,
    row_sent,
    row_got,
    meta_sent,
    meta_got,
    halo_sent,
    halo_got,
):
    loads = [
        pltpu.make_async_copy(source, target, loaded.at[i])
        for i, (source, target) in enumerate(
            (
                (owner_hbm, owner_ref),
                (slot_hbm, slot_ref),
                (live_hbm, live_ref),
                (rows_hbm, rows_ref),
                (gain_hbm, gain_ref),
                (bias_hbm, bias_ref),
                (out_bias_hbm, out_bias_ref),
            )
        )
    ]
    for load in loads:
        load.start()
    rows, channels = rows_ref.shape
    out_width = out_bias_ref.shape[1]
    weight_loads = [
        pltpu.make_async_copy(
            weight_hbm.at[a * 3 + b, pl.ds(d * channels, channels)],
            weight_ref.at[b, pl.ds(a * channels, channels), pl.ds(d * out_width, out_width)],
            weight_loaded.at[(a * 3 + b) * 3 + d],
        )
        for a in range(3)
        for b in range(3)
        for d in range(3)
    ]
    count = tiles * clips
    joint = joint_of(count, cap)
    depth = bits(count)
    half = count // 2
    quarter = count // 4
    own = half
    my_tile = lax.axis_index("tile")
    my_clip = lax.axis_index("clip")
    me = my_tile * clips + my_clip
    far = me // half
    odd = (me // quarter) % 2

    signs = [1 - 2 * ((me // (1 << i)) % 2) for i in range(depth)]
    low_bits = bits(clips)

    def other(mask):
        tile, clip = my_tile, my_clip
        for i in range(depth):
            bit = (mask // (1 << i)) % 2
            if isinstance(bit, int) and not bit:
                continue
            if i < low_bits:
                clip = clip + bit * signs[i] * (1 << i)
            else:
                tile = tile + bit * signs[i] * (1 << (i - low_bits))
        return tile, clip

    def mask_of(k):
        crossing = 1 - k // half
        low = k % half
        if isinstance(k, int):
            bit = low // quarter
            swap = bit + (1 - 2 * bit) * crossing * odd
        else:
            swap = (low // quarter + crossing * odd) % 2
        return crossing * half + low % quarter, swap * quarter

    def partner(k):
        mask, extra = mask_of(k)
        tile, clip = other(mask)
        i = depth - 2
        tile = tile + (extra // quarter) * signs[i] * (1 << (i - low_bits))
        return mask + extra, (tile, clip)

    def each(begin, end, step):
        if end - begin <= 32:
            for k in range(begin, end):
                step(k)
        else:
            pl.loop(begin, end)(step)

    def unless(condition, step):
        if isinstance(condition, bool):
            if not condition:
                step()
        else:
            pl.when(jnp.logical_not(condition))(step)

    barrier = pltpu.get_barrier_semaphore()

    def announce(mask):
        pl.semaphore_signal(barrier, inc=1, device_id=other(mask), device_id_type=MESH)

    each(1, count, announce)

    for buffer in (edge_in, face_in, corner_in, volume, side):
        buffer[...] = jnp.zeros_like(buffer)
    chunks = rows // LANES
    before = (iota((LANES, 2 * LANES), 0) < iota((LANES, 2 * LANES), 1)).astype(F32).astype(BF16)
    for load in loads[:2]:
        load.wait()
    owner = owner_ref[...]
    slot = slot_ref[...]
    to_clip = owner >> bits(tiles)
    mask = ((owner & (tiles - 1)) * clips + to_clip) ^ me
    crossing = mask >> (depth - 1)
    order = mask ^ half ^ (crossing * (odd * quarter))
    table = (iota((count, rows), 0) == order).astype(F32)
    table16 = table.astype(BF16)
    stacked = jnp.concatenate([table16[:, c * LANES : (c + 1) * LANES] for c in range(chunks)], axis=0)
    counted = dot(stacked, before)
    base = jnp.zeros((count, LANES), F32)
    ranks = []
    for c in range(chunks):
        part = counted[c * count : (c + 1) * count]
        hit = table[:, c * LANES : (c + 1) * LANES]
        ranks.append(jnp.sum((part[:, :LANES] + base) * hit, axis=0, keepdims=True))
        base = base + part[:, LANES:]
    rank = jnp.concatenate(ranks, axis=1).astype(jnp.int32)
    position = order * cap + rank

    label = slot + 1
    by_rank = (iota((LANES, rows), 0) == rank).astype(F32).astype(BF16)
    digits = jnp.concatenate(
        [table * (label >> 5).astype(F32), table * (label & 31).astype(F32)], axis=0
    ).astype(BF16)
    labels = lax.dot_general(digits, by_rank, NT, preferred_element_type=F32)
    labels = labels[:count] * 32.0 + labels[count:]

    for load in loads[2:4]:
        load.wait()
    for load in weight_loads:
        load.start()
    values = rows_ref[...]
    per_group = bits(channels // GROUPS)

    def partial_sums():
        clip_row = iota((8, rows), 0)
        live_limit = jnp.zeros((8, rows), jnp.int32)
        for c in range(clips):
            live_limit = jnp.where(clip_row == c, live_ref[c] * PLANE, live_limit)
        live_row = ((clip_row == to_clip) & (slot < live_limit)).astype(F32).astype(BF16)
        wide = values.astype(F32)
        square = wide * wide
        high = square.astype(BF16)
        low = (square - high.astype(F32)).astype(BF16)
        sum1 = dot(live_row, values)
        sum2 = dot(live_row, high) + dot(live_row, low)
        group = iota((channels, LANES), 0) >> per_group
        lane = iota((channels, LANES), 1)
        partial = dot(sum1, (lane - STAT == group).astype(F32), precision=HIGHEST) + dot(
            sum2, (lane - STAT - GROUPS == group).astype(F32), precision=HIGHEST
        )
        goes = (my_clip ^ iota((count, LANES), 0)) & (clips - 1)
        stats = jnp.zeros((count, LANES), F32)
        for c in range(clips):
            stats = jnp.where(goes == c, partial[c : c + 1], stats)
        return stats

    def row_copy(k):
        mask, device = partner(k)
        return pltpu.make_async_remote_copy(
            src_ref=send_rows.at[k],
            dst_ref=recv_rows.at[mask],
            send_sem=row_sent,
            recv_sem=row_got.at[mask // joint],
            device_id=device,
            device_id_type=MESH,
        )

    def meta_copy(k):
        mask, device = partner(k)
        return pltpu.make_async_remote_copy(
            src_ref=send_meta.at[k],
            dst_ref=recv_meta.at[mask],
            send_sem=meta_sent,
            recv_sem=meta_got,
            device_id=device,
            device_id_type=MESH,
        )

    batch = max(1, min(quarter // 2, 256 // cap))
    while quarter % batch:
        batch -= 1

    def pack(first, size):
        chosen = (iota((size * cap, rows), 0) + first * cap == position).astype(F32).astype(BF16)
        packed = dot(chosen, values).astype(BF16)
        send_rows[first : first + size] = packed.reshape(size, cap, channels)

    def start_rows(begin, end):
        def step(k):
            row_copy(k).start()
            unless(k == 0, lambda: row_copy(half + k).start())

        each(begin, end, step)

    pack(0, batch)
    pack(half, batch)
    pl.semaphore_wait(barrier, count - 1)
    start_rows(0, batch)
    metas = labels + partial_sums()
    for k in range(count):
        send_meta[k] = metas[k : k + 1]
    recv_meta[0] = send_meta[own]
    each(0, count, lambda k: unless(k == own, lambda: meta_copy(k).start()))
    for first, last in ((batch, quarter), (quarter, half)):
        pack(first, last - first)
        pack(half + first, last - first)
        start_rows(first, last)
    recv_rows[0] = send_rows[own]

    def all_metas():
        return pltpu.make_async_remote_copy(
            src_ref=send_meta.at[pl.ds(0, count - 1)],
            dst_ref=recv_meta.at[pl.ds(1, count - 1)],
            send_sem=meta_sent,
            recv_sem=meta_got,
            device_id=other(1),
            device_id_type=MESH,
        )

    def some_rows(q, first, blocks):
        return pltpu.make_async_remote_copy(
            src_ref=send_rows.at[pl.ds(0, blocks)],
            dst_ref=recv_rows.at[pl.ds(first, blocks)],
            send_sem=row_sent,
            recv_sem=row_got.at[q],
            device_id=other(1),
            device_id_type=MESH,
        )

    all_metas().wait_recv()

    width = joint * cap
    groups = count // joint
    metas_in = jnp.concatenate([recv_meta[m] for m in range(count)], axis=0)
    spread_lane = iota((LANES, width), 0)
    spread_col = iota((LANES, width), 1)
    spread = jnp.zeros((LANES, width), F32)
    block_of = jnp.zeros((count, width), jnp.int32)
    for m in range(joint):
        spread = jnp.where((spread_col - m * cap == spread_lane) & (spread_lane < cap), 1.0, spread)
        block_of = jnp.where(iota((count, width), 1) >= m * cap, m, block_of)
    moved = dot(metas_in, spread, precision=HIGHEST)
    source_of = iota((count, width), 0)
    for q in range(groups):
        keep = source_of == block_of + q * joint
        row = jnp.sum(jnp.where(keep, moved, 0.0), axis=0, keepdims=True)
        slots_ref[q] = (row + 0.5).astype(jnp.int32) - 1

    for load in loads[4:]:
        load.wait()
    live = live_ref[my_clip]
    sums_in = jnp.broadcast_to(jnp.sum(metas_in, axis=0, keepdims=True), (8, LANES))
    voxels = jnp.full((8, LANES), live * ((channels // GROUPS) * PLANE * tiles), jnp.int32)
    scaled = sums_in / voxels.astype(F32)
    stat_lane = iota((LANES, channels), 0)
    stat_group = iota((LANES, channels), 1) >> per_group
    mean = dot(scaled, (stat_lane - STAT == stat_group).astype(F32), precision=HIGHEST)
    second = dot(scaled, (stat_lane - STAT - GROUPS == stat_group).astype(F32), precision=HIGHEST)
    scale = lax.rsqrt(second - mean * mean + EPSILON)
    scale = (0.5 * (scale * gain_ref[...]))[0:1]
    mean = mean[0:1]
    bias = 0.5 * bias_ref[...]

    def activate(raw):
        u = (raw.astype(F32) - mean) * scale + bias
        return (u + u * jnp.tanh(u)).astype(BF16)

    edge_row = iota((EDGE, width), 0)
    edge_line = (edge_row >> bits(2 * TH)) * TH + (edge_row & (TH - 1))
    edge_voxel = edge_line * TW + jnp.where((edge_row & TH) == 0, TW - 1, 0)
    voxel = jnp.concatenate([iota((rows, width), 0), edge_voxel], axis=0)

    def place(q, blocks=joint):
        some_rows(q, q * joint + joint - blocks, blocks).wait_recv()
        target = (voxel == slots_ref[q]).astype(F32).astype(BF16)
        arrived = recv_rows[pl.ds(q * joint, joint)].reshape(width, channels)
        return dot(target, activate(arrived)).astype(BF16)

    half_groups = groups // 2
    quarter_groups = groups // 4
    flip = (odd + 1 - far) % 2

    def group_of(p):
        late = p // half_groups
        low = p % half_groups
        swap = (low // quarter_groups + late * flip) % 2
        return late * half_groups + swap * quarter_groups + low % quarter_groups

    placed_ref[...] = place(0, joint - 1)

    @pl.loop(1, groups - 1)
    def _(p):
        placed_ref[...] += place(group_of(p))

    tile = placed_ref[...] + place(group_of(groups - 1))
    edge_out[...] = tile[rows:]
    grid = tile[:rows].reshape(LT, TH, TW, channels)
    for a in range(3):
        volume[2 - a :, 1 : TH + 1, :, a * channels : (a + 1) * channels] = grid[: LT - 2 + a]

    grid_rows = tiles // GW
    row_tile = my_tile // GW
    column_tile = my_tile % GW

    def exists(down, right):
        row = row_tile + down
        column = column_tile + right
        return (row >= 0) & (row < grid_rows) & (column >= 0) & (column < GW)

    def halo_copy(e):
        down, right = EDGES[e]
        if e < 2:
            return pltpu.make_async_remote_copy(
                src_ref=edge_out,
                dst_ref=edge_in.at[e],
                send_sem=halo_sent.at[e],
                recv_sem=halo_got.at[e],
                device_id=(my_tile + right, my_clip),
                device_id_type=MESH,
            )
        if e < 4:
            part, source_ref, target_ref = e - 2, face_out, face_in
        else:
            part, source_ref, target_ref = e - 4, corner_out, corner_in
        return pltpu.make_async_remote_copy(
            src_ref=source_ref.at[part],
            dst_ref=target_ref.at[part],
            send_sem=halo_sent.at[e],
            recv_sem=halo_got.at[e],
            device_id=(my_tile + down * GW + right, my_clip),
            device_id_type=MESH,
        )

    def send(e):
        @pl.when(exists(*EDGES[e]))
        def _():
            halo_copy(e).start()

    def receive(e):
        down, right = EDGES[e]

        @pl.when(exists(-down, -right))
        def _():
            halo_copy(e).wait_recv()

    send(0)
    send(1)
    for load in weight_loads:
        load.wait()

    def shifted(product, column):
        taps = [product[:, d * out_width : (d + 1) * out_width] for d in range(3)]
        n = product.shape[0]
        after = jnp.where(column == 0, 0.0, pltpu.roll(taps[0], 1, 0))
        ahead = jnp.where(column == TW - 1, 0.0, pltpu.roll(taps[2], n - 1, 0))
        return after + taps[1] + ahead

    lines = LT * TW
    line_column = iota((lines, out_width), 0) & (TW - 1)
    for f in range(2):
        @pl.when(exists(1 - 2 * f, 0))
        def _():
            b, h = (0, TH) if f == 0 else (2, 1)
            outer = dot(volume[:, h].reshape(lines, 3 * channels), weight_ref[b])
            face_out[f] = shifted(outer, line_column).astype(BF16)
            send(2 + f)
            by_frame = outer.reshape(LT, TW, 3 * out_width)
            for g in range(2):
                w, d = (TW - 1, 0) if g == 0 else (0, 2)
                corner = by_frame[:, w, d * out_width : (d + 1) * out_width]
                corner_out[2 * f + g] = jnp.concatenate(
                    [corner[:, : out_width // 2], corner[:, out_width // 2 :]], axis=0
                )
                send(4 + 2 * f + g)

    plane_column = iota((PLANE, out_width), 0) & (TW - 1)

    out_bias = out_bias_ref[...]

    def frame_sum(t, extra):
        skip = max(0, 2 - t) * channels
        product = None
        beside = []
        for b in range(3):
            slab = volume[t, b : b + TH, :, skip:].reshape(PLANE, 3 * channels - skip)
            if extra:
                slab = jnp.concatenate([slab, side[...].reshape(EDGE, 3 * channels)], axis=0)
            term = dot(slab, weight_ref[b, skip:])
            product = term[:PLANE] if product is None else product + term[:PLANE]
            beside.append(term[PLANE:])
        summed[t] = shifted(product, plane_column) + out_bias
        return beside

    for t in range(LT - 1):
        frame_sum(t, False)
    receive(0)
    receive(1)
    from_left = (iota((EDGE, channels), 0) & TH) == 0
    edges = jnp.where(from_left, edge_in[0].astype(F32), edge_in[1].astype(F32))
    edges = edges.astype(BF16).reshape(LT, 2 * TH, channels)
    for a in range(3):
        side[2 - a :, :, a * channels : (a + 1) * channels] = edges[: LT - 2 + a]
    from_left = (iota((EDGE, out_width), 0) & TH) == 0
    line = iota((EDGE, out_width), 0) & (TH - 1)
    taps = [
        jnp.where(from_left, term[:, :out_width], term[:, 2 * out_width :])
        for term in frame_sum(LT - 1, True)
    ]
    beside = (
        jnp.where(line == 0, 0.0, pltpu.roll(taps[0], 1, 0))
        + taps[1]
        + jnp.where(line == TH - 1, 0.0, pltpu.roll(taps[2], EDGE - 1, 0))
    )
    for e in range(2, 8):
        receive(e)

    strip = TW // 2
    column = iota((strip, out_width), 0)

    def corner_of(i, t):
        return jnp.concatenate([corner_in[i, t : t + 1], corner_in[i, LT + t : LT + t + 1]], axis=1)

    for t in range(LT):
        for h in range(TH):
            for g in range(2):
                n = t * 2 * TH + g * TH + h
                extra = beside[n : n + 1]
                total = summed[t, h * TW + g * strip : h * TW + (g + 1) * strip]
                if h in (0, TH - 1):
                    f = 0 if h == 0 else 1
                    begin = t * TW + g * strip
                    total = total + face_in[f, begin : begin + strip].astype(F32)
                    extra = extra + corner_of(2 * f + g, t)
                total = total + jnp.where(column == g * (strip - 1), extra, 0.0)
                begin = (t * TH + h) * TW + g * strip
                out_ref[begin : begin + strip] = jnp.where(t < live, total, 0.0).astype(BF16)

    all_metas().wait_send()
    some_rows(0, 1, count - 1).wait_send()

    for e, (down, right) in enumerate(EDGES):
        @pl.when(exists(down, right))
        def _():
            halo_copy(e).wait_send()


def on_device(
    seq_rows, plan_owner, plan_slot, live_frames, norm_gain, norm_bias, conv_weight, conv_bias
):
    rows, channels = seq_rows.shape
    out_width = conv_bias.shape[0]
    tiles = lax.axis_size("tile")
    clips = lax.axis_size("clip")
    count = tiles * clips
    cap = -(-(3 * (rows // count) // 2) // 16) * 16
    joint = joint_of(count, cap)
    dma = pltpu.SemaphoreType.DMA
    decoded = pl.pallas_call(
        functools.partial(decode_kernel, tiles, clips, cap),
        out_shape=pltpu.VMEM((rows, out_width), BF16),
        in_specs=[pl.BlockSpec(memory_space=pltpu.HBM)] * 8,
        out_specs=pl.BlockSpec(memory_space=pltpu.VMEM),
        scratch_shapes=[
            pltpu.SMEM((clips,), jnp.int32),
            pltpu.VMEM((1, rows), jnp.int32),
            pltpu.VMEM((1, rows), jnp.int32),
            pltpu.VMEM((rows, channels), BF16),
            pltpu.VMEM((1, channels), F32),
            pltpu.VMEM((1, channels), F32),
            pltpu.VMEM((1, out_width), F32),
            pltpu.VMEM((3, 3 * channels, 3 * out_width), BF16),
            pltpu.VMEM((count, cap, channels), BF16),
            pltpu.VMEM((count, cap, channels), BF16),
            pltpu.VMEM((count, 1, LANES), F32),
            pltpu.VMEM((count, 1, LANES), F32),
            pltpu.VMEM((count // joint, 1, joint * cap), jnp.int32),
            pltpu.VMEM((rows + EDGE, channels), BF16),
            pltpu.VMEM((LT, TH + 2, TW, 3 * channels), BF16),
            pltpu.VMEM((LT, 2 * TH, 3 * channels), BF16),
            pltpu.VMEM((EDGE, channels), BF16),
            pltpu.VMEM((2, EDGE, channels), BF16),
            pltpu.VMEM((2, LT * TW, out_width), BF16),
            pltpu.VMEM((2, LT * TW, out_width), BF16),
            pltpu.VMEM((4, 2 * LT, out_width // 2), F32),
            pltpu.VMEM((4, 2 * LT, out_width // 2), F32),
            pltpu.VMEM((LT, PLANE, out_width), F32),
            dma((7,)),
            dma((27,)),
            dma,
            dma((count // joint,)),
            dma,
            dma,
            dma((8,)),
            dma((8,)),
        ],
        compiler_params=pltpu.CompilerParams(
            collective_id=0, has_side_effects=True, vmem_limit_bytes=56 << 20
        ),
        name="decode",
    )(
        live_frames,
        plan_owner.reshape(1, rows),
        plan_slot.reshape(1, rows),
        seq_rows,
        norm_gain.reshape(1, channels),
        norm_bias.reshape(1, channels),
        conv_bias.reshape(1, out_width),
        conv_weight.transpose(0, 1, 3, 2, 4).reshape(9, 3 * channels, out_width),
    )

    def finish(held_ref, result_ref, done):
        copy = pltpu.make_async_copy(held_ref, result_ref, done)
        copy.start()
        copy.wait()

    decoded = pl.pallas_call(
        finish,
        out_shape=jax.ShapeDtypeStruct((rows, out_width), BF16),
        in_specs=[pl.BlockSpec(memory_space=pltpu.VMEM)],
        out_specs=pl.BlockSpec(memory_space=pltpu.HBM),
        scratch_shapes=[dma],
        name="finish",
    )(pltpu.with_memory_space_constraint(decoded, pltpu.VMEM))
    return decoded.reshape(1, 1, LT, TH, TW, out_width)


def solution(mesh):
    return jax.shard_map(
        on_device,
        mesh=mesh,
        in_specs=(
            P(("tile", "clip"), None),
            P(("tile", "clip")),
            P(("tile", "clip")),
            P(),
            P(),
            P(),
            P(),
            P(),
        ),
        out_specs=P("clip", "tile", None, None, None, None),
        check_vma=False,
    )
```

```python
import functools

import jax
import jax.numpy as jnp
from jax import lax
from jax.experimental import pallas as pl
from jax.experimental.pallas import tpu as pltpu
from jax.sharding import PartitionSpec as P

GROUPS = 32
LT = 4
TH = 8
TW = 32
GW = 4
PLANE = TH * TW
LANES = 128
STAT = 64
EDGE = 2 * LT * TH
EPSILON = 1e-06
HIGHEST = lax.Precision.HIGHEST
F32 = jnp.float32
BF16 = jnp.bfloat16
NT = (((1,), (1,)), ((), ()))
MESH = pl.DeviceIdType.MESH
EDGES = ((0, 1), (0, -1), (1, 0), (-1, 0), (1, 1), (1, -1), (-1, 1), (-1, -1))


def iota(shape, axis):
    return lax.broadcasted_iota(jnp.int32, shape, axis)


def bits(n):
    return n.bit_length() - 1


def dot(a, b, **kw):
    return jnp.dot(a, b, preferred_element_type=F32, **kw)


def joint_of(count, cap):
    joint = max(1, min(count // 4, 128 // cap))
    while (count // 4) % joint:
        joint -= 1
    return joint


def decode_kernel(
    tiles,
    clips,
    cap,
    live_hbm,
    owner_hbm,
    slot_hbm,
    rows_hbm,
    gain_hbm,
    bias_hbm,
    out_bias_hbm,
    weight_hbm,
    out_ref,
    live_ref,
    owner_ref,
    slot_ref,
    rows_ref,
    gain_ref,
    bias_ref,
    out_bias_ref,
    weight_ref,
    send_rows,
    recv_rows,
    send_meta,
    recv_meta,
    slots_ref,
    placed_ref,
    volume,
    side,
    edge_out,
    edge_in,
    face_out,
    face_in,
    corner_out,
    corner_in,
    summed,
    loaded,
    weight_loaded,
    row_sent,
    row_got,
    meta_sent,
    meta_got,
    halo_sent,
    halo_got,
):
    loads = [
        pltpu.make_async_copy(source, target, loaded.at[i])
        for i, (source, target) in enumerate(
            (
                (owner_hbm, owner_ref),
                (slot_hbm, slot_ref),
                (live_hbm, live_ref),
                (rows_hbm, rows_ref),
                (gain_hbm, gain_ref),
                (bias_hbm, bias_ref),
                (out_bias_hbm, out_bias_ref),
            )
        )
    ]
    rows, channels = rows_ref.shape
    out_width = out_bias_ref.shape[1]
    weight_loads = [
        pltpu.make_async_copy(
            weight_hbm.at[a * 3 + b, pl.ds(d * channels, channels)],
            weight_ref.at[b, pl.ds(a * channels, channels), pl.ds(d * out_width, out_width)],
            weight_loaded,
        )
        for a in range(3)
        for b in range(3)
        for d in range(3)
    ]
    count = tiles * clips
    joint = joint_of(count, cap)
    depth = bits(count)
    half = count // 2
    quarter = count // 4
    own = half
    my_tile = lax.axis_index("tile")
    my_clip = lax.axis_index("clip")
    me = my_tile * clips + my_clip
    far = me // half
    odd = (me // quarter) % 2

    signs = [1 - 2 * ((me // (1 << i)) % 2) for i in range(depth)]
    low_bits = bits(clips)

    def other(mask):
        tile, clip = my_tile, my_clip
        for i in range(depth):
            bit = (mask // (1 << i)) % 2
            if isinstance(bit, int) and not bit:
                continue
            if i < low_bits:
                clip = clip + bit * signs[i] * (1 << i)
            else:
                tile = tile + bit * signs[i] * (1 << (i - low_bits))
        return tile, clip

    def mask_of(k):
        crossing = 1 - k // half
        low = k % half
        if isinstance(k, int):
            bit = low // quarter
            swap = bit + (1 - 2 * bit) * crossing * odd
        else:
            swap = (low // quarter + crossing * odd) % 2
        return crossing * half + low % quarter, swap * quarter

    def partner(k):
        mask, extra = mask_of(k)
        tile, clip = other(mask)
        i = depth - 2
        tile = tile + (extra // quarter) * signs[i] * (1 << (i - low_bits))
        return mask + extra, (tile, clip)

    def each(begin, end, step):
        if end - begin <= 32:
            for k in range(begin, end):
                step(k)
        else:
            pl.loop(begin, end)(step)

    def unless(condition, step):
        if isinstance(condition, bool):
            if not condition:
                step()
        else:
            pl.when(jnp.logical_not(condition))(step)

    barrier = pltpu.get_barrier_semaphore()

    def announce(mask):
        pl.semaphore_signal(barrier, inc=1, device_id=other(count - mask), device_id_type=MESH)

    for load in loads[:2]:
        load.start()
    each(1, count, announce)
    for load in loads[2:]:
        load.start()

    for buffer in (edge_in, face_in, corner_in, volume, side):
        buffer[...] = jnp.zeros_like(buffer)
    chunks = rows // LANES
    before = (iota((LANES, 2 * LANES), 0) < iota((LANES, 2 * LANES), 1)).astype(F32).astype(BF16)
    for load in loads[:2]:
        load.wait()
    owner = owner_ref[...]
    slot = slot_ref[...]
    to_clip = owner >> bits(tiles)
    mask = ((owner & (tiles - 1)) * clips + to_clip) ^ me
    crossing = mask >> (depth - 1)
    order = mask ^ half ^ (crossing * (odd * quarter))
    table = (iota((count, rows), 0) == order).astype(F32)
    table16 = table.astype(BF16)
    stacked = jnp.concatenate([table16[:, c * LANES : (c + 1) * LANES] for c in range(chunks)], axis=0)
    counted = dot(stacked, before)
    base = jnp.zeros((count, LANES), F32)
    ranks = []
    for c in range(chunks):
        part = counted[c * count : (c + 1) * count]
        hit = table[:, c * LANES : (c + 1) * LANES]
        ranks.append(jnp.sum((part[:, :LANES] + base) * hit, axis=0, keepdims=True))
        base = base + part[:, LANES:]
    rank = jnp.concatenate(ranks, axis=1).astype(jnp.int32)
    position = order * cap + rank

    label = slot + 1
    by_rank = (iota((LANES, rows), 0) == rank).astype(F32).astype(BF16)
    digits = jnp.concatenate(
        [table * (label >> 5).astype(F32), table * (label & 31).astype(F32)], axis=0
    ).astype(BF16)
    labels = lax.dot_general(digits, by_rank, NT, preferred_element_type=F32)
    labels = labels[:count] * 32.0 + labels[count:]

    for load in loads[2:4]:
        load.wait()
    for load in weight_loads:
        load.start()
    values = rows_ref[...]
    per_group = bits(channels // GROUPS)

    def partial_sums():
        clip_row = iota((8, rows), 0)
        live_limit = jnp.zeros((8, rows), jnp.int32)
        for c in range(clips):
            live_limit = jnp.where(clip_row == c, live_ref[c] * PLANE, live_limit)
        live_row = ((clip_row == to_clip) & (slot < live_limit)).astype(F32).astype(BF16)
        wide = values.astype(F32)
        square = wide * wide
        high = square.astype(BF16)
        low = (square - high.astype(F32)).astype(BF16)
        sum1 = dot(live_row, values)
        sum2 = dot(live_row, high) + dot(live_row, low)
        group = iota((channels, LANES), 0) >> per_group
        lane = iota((channels, LANES), 1)
        partial = dot(sum1, (lane - STAT == group).astype(F32), precision=HIGHEST) + dot(
            sum2, (lane - STAT - GROUPS == group).astype(F32), precision=HIGHEST
        )
        goes = (my_clip ^ iota((count, LANES), 0)) & (clips - 1)
        stats = jnp.zeros((count, LANES), F32)
        for c in range(clips):
            stats = jnp.where(goes == c, partial[c : c + 1], stats)
        return stats

    def row_copy(k):
        mask, device = partner(k)
        return pltpu.make_async_remote_copy(
            src_ref=send_rows.at[k],
            dst_ref=recv_rows.at[mask],
            send_sem=row_sent,
            recv_sem=row_got.at[mask // joint],
            device_id=device,
            device_id_type=MESH,
        )

    def meta_copy(k):
        mask, device = partner(k)
        return pltpu.make_async_remote_copy(
            src_ref=send_meta.at[k],
            dst_ref=recv_meta.at[mask],
            send_sem=meta_sent,
            recv_sem=meta_got,
            device_id=device,
            device_id_type=MESH,
        )

    batch = max(1, min(quarter // 2, 256 // cap))
    while quarter % batch:
        batch -= 1

    def pack(first, size):
        chosen = (iota((size * cap, rows), 0) + first * cap == position).astype(F32).astype(BF16)
        packed = dot(chosen, values).astype(BF16)
        send_rows[first : first + size] = packed.reshape(size, cap, channels)

    def start_rows(begin, end):
        def step(k):
            row_copy(k).start()
            unless(k == 0, lambda: row_copy(half + k).start())

        each(begin, end, step)

    pack(0, batch)
    pack(half, batch)
    pl.semaphore_wait(barrier, count - 1)
    start_rows(0, batch)
    metas = labels + partial_sums()
    for k in range(count):
        send_meta[k] = metas[k : k + 1]
    recv_meta[0] = send_meta[own]
    each(0, count, lambda k: unless(k == own, lambda: meta_copy(k).start()))
    for first, last in ((batch, quarter), (quarter, half)):
        pack(first, last - first)
        pack(half + first, last - first)
        start_rows(first, last)
    recv_rows[0] = send_rows[own]

    def all_metas():
        return pltpu.make_async_remote_copy(
            src_ref=send_meta.at[pl.ds(0, count - 1)],
            dst_ref=recv_meta.at[pl.ds(1, count - 1)],
            send_sem=meta_sent,
            recv_sem=meta_got,
            device_id=other(1),
            device_id_type=MESH,
        )

    def some_rows(q, first, blocks):
        return pltpu.make_async_remote_copy(
            src_ref=send_rows.at[pl.ds(0, blocks)],
            dst_ref=recv_rows.at[pl.ds(first, blocks)],
            send_sem=row_sent,
            recv_sem=row_got.at[q],
            device_id=other(1),
            device_id_type=MESH,
        )

    all_metas().wait_recv()

    width = joint * cap
    groups = count // joint
    metas_in = jnp.concatenate([recv_meta[m] for m in range(count)], axis=0)
    spread_lane = iota((LANES, width), 0)
    spread_col = iota((LANES, width), 1)
    spread = jnp.zeros((LANES, width), F32)
    block_of = jnp.zeros((count, width), jnp.int32)
    for m in range(joint):
        spread = jnp.where((spread_col - m * cap == spread_lane) & (spread_lane < cap), 1.0, spread)
        block_of = jnp.where(iota((count, width), 1) >= m * cap, m, block_of)
    moved = dot(metas_in, spread, precision=HIGHEST)
    source_of = iota((count, width), 0)
    for q in range(groups):
        keep = source_of == block_of + q * joint
        row = jnp.sum(jnp.where(keep, moved, 0.0), axis=0, keepdims=True)
        slots_ref[q] = (row + 0.5).astype(jnp.int32) - 1

    for load in loads[4:]:
        load.wait()
    live = live_ref[my_clip]
    sums_in = jnp.broadcast_to(jnp.sum(metas_in, axis=0, keepdims=True), (8, LANES))
    voxels = jnp.full((8, LANES), live * ((channels // GROUPS) * PLANE * tiles), jnp.int32)
    scaled = sums_in / voxels.astype(F32)
    stat_lane = iota((LANES, channels), 0)
    stat_group = iota((LANES, channels), 1) >> per_group
    mean = dot(scaled, (stat_lane - STAT == stat_group).astype(F32), precision=HIGHEST)
    second = dot(scaled, (stat_lane - STAT - GROUPS == stat_group).astype(F32), precision=HIGHEST)
    scale = lax.rsqrt(second - mean * mean + EPSILON)
    scale = (0.5 * (scale * gain_ref[...]))[0:1]
    mean = mean[0:1]
    bias = 0.5 * bias_ref[...]

    def activate(raw):
        u = (raw.astype(F32) - mean) * scale + bias
        return (u + u * jnp.tanh(u)).astype(BF16)

    edge_row = iota((EDGE, width), 0)
    edge_voxel = edge_row * TW + jnp.where(edge_row < EDGE // 2, TW - 1, -rows)
    voxel = jnp.concatenate([iota((rows, width), 0), edge_voxel], axis=0)

    def gather(q, blocks=joint):
        some_rows(q, q * joint + joint - blocks, blocks).wait_recv()
        return activate(recv_rows[pl.ds(q * joint, joint)].reshape(width, channels))

    def move(targets, q, arrived):
        return dot((targets == slots_ref[q]).astype(F32).astype(BF16), arrived).astype(BF16)

    half_groups = groups // 2
    quarter_groups = groups // 4
    flip = (odd + 1 - far) % 2

    def group_of(p):
        late = p // half_groups
        low = p % half_groups
        swap = (low // quarter_groups + late * flip) % 2
        return late * half_groups + swap * quarter_groups + low % quarter_groups

    placed_ref[...] = move(voxel, 0, gather(0, joint - 1))

    @pl.loop(1, groups - 1)
    def _(p):
        q = group_of(p)
        placed_ref[...] += move(voxel, q, gather(q))

    grid_rows = tiles // GW
    row_tile = my_tile // GW
    column_tile = my_tile % GW

    def exists(down, right):
        row = row_tile + down
        column = column_tile + right
        return (row >= 0) & (row < grid_rows) & (column >= 0) & (column < GW)

    def halo_copy(e):
        down, right = EDGES[e]
        if e < 2:
            part, source_ref, target_ref = pl.ds(e * (EDGE // 2), EDGE // 2), edge_out, edge_in
        elif e < 4:
            part, source_ref, target_ref = e - 2, face_out, face_in
        else:
            part, source_ref, target_ref = e - 4, corner_out, corner_in
        return pltpu.make_async_remote_copy(
            src_ref=source_ref.at[part],
            dst_ref=target_ref.at[part],
            send_sem=halo_sent.at[e],
            recv_sem=halo_got.at[e],
            device_id=(my_tile + down * GW + right, my_clip),
            device_id_type=MESH,
        )

    def send(e):
        @pl.when(exists(*EDGES[e]))
        def _():
            halo_copy(e).start()

    def receive(e):
        down, right = EDGES[e]

        @pl.when(exists(-down, -right))
        def _():
            halo_copy(e).wait_recv()

    pltpu.make_async_copy(weight_ref, weight_ref, weight_loaded).wait()
    final = group_of(groups - 1)
    tile = placed_ref[...] + move(voxel, final, gather(final))
    edge_out[...] = tile[rows:]
    send(0)
    send(1)
    grid = tile[:rows].reshape(LT, TH, TW, channels)
    for a in range(3):
        volume[2 - a :, 1 : TH + 1, :, a * channels : (a + 1) * channels] = grid[: LT - 2 + a]

    def shifted(product, column):
        taps = [product[:, d * out_width : (d + 1) * out_width] for d in range(3)]
        n = product.shape[0]
        after = jnp.where(column == 0, 0.0, pltpu.roll(taps[0], 1, 0))
        ahead = jnp.where(column == TW - 1, 0.0, pltpu.roll(taps[2], n - 1, 0))
        return after + taps[1] + ahead

    lines = LT * TW
    line_column = iota((lines, out_width), 0) & (TW - 1)
    for f in range(2):
        @pl.when(exists(1 - 2 * f, 0))
        def _():
            b, h = (0, TH) if f == 0 else (2, 1)
            outer = dot(volume[:, h].reshape(lines, 3 * channels), weight_ref[b])
            by_frame = outer.reshape(LT, TW, 3 * out_width)
            for g in range(2):
                w, d = (TW - 1, 0) if g == 0 else (0, 2)
                corner = by_frame[:, w, d * out_width : (d + 1) * out_width]
                corner_out[2 * f + g] = jnp.concatenate(
                    [corner[:, : out_width // 2], corner[:, out_width // 2 :]], axis=0
                )
                send(4 + 2 * f + g)
            face_out[f] = shifted(outer, line_column).astype(BF16)
            send(2 + f)

    plane_column = iota((PLANE, out_width), 0) & (TW - 1)

    out_bias = out_bias_ref[...]

    def frame_sum(t, extra):
        skip = max(0, 2 - t) * channels
        product = None
        beside = []
        for b in range(3):
            slab = volume[t, b : b + TH, :, skip:].reshape(PLANE, 3 * channels - skip)
            if extra:
                slab = jnp.concatenate([slab, side[...].reshape(EDGE, 3 * channels)], axis=0)
            term = dot(slab, weight_ref[b, skip:])
            product = term[:PLANE] if product is None else product + term[:PLANE]
            beside.append(term[PLANE:])
        summed[t] = shifted(product, plane_column) + out_bias
        return beside

    for t in range(LT - 1):
        frame_sum(t, False)
    receive(0)
    receive(1)
    edges = edge_in[...].astype(F32)
    edges = jnp.concatenate(
        [edges[n * TH : (n + 1) * TH] for t in range(LT) for n in (t, LT + t)], axis=0
    ).astype(BF16)
    edges = edges.reshape(LT, 2 * TH, channels)
    for a in range(3):
        side[2 - a :, :, a * channels : (a + 1) * channels] = edges[: LT - 2 + a]
    from_left = (iota((EDGE, out_width), 0) & TH) == 0
    line = iota((EDGE, out_width), 0) & (TH - 1)
    taps = [
        jnp.where(from_left, term[:, :out_width], term[:, 2 * out_width :])
        for term in frame_sum(LT - 1, True)
    ]
    beside = (
        jnp.where(line == 0, 0.0, pltpu.roll(taps[0], 1, 0))
        + taps[1]
        + jnp.where(line == TH - 1, 0.0, pltpu.roll(taps[2], EDGE - 1, 0))
    )
    for e in range(2, 8):
        receive(e)

    strip = TW // 2
    column = iota((strip, out_width), 0)

    def corner_of(i, t):
        return jnp.concatenate([corner_in[i, t : t + 1], corner_in[i, LT + t : LT + t + 1]], axis=1)

    for t in range(LT):
        for h in range(TH):
            for g in range(2):
                n = t * 2 * TH + g * TH + h
                extra = beside[n : n + 1]
                total = summed[t, h * TW + g * strip : h * TW + (g + 1) * strip]
                if h in (0, TH - 1):
                    f = 0 if h == 0 else 1
                    begin = t * TW + g * strip
                    total = total + face_in[f, begin : begin + strip].astype(F32)
                    extra = extra + corner_of(2 * f + g, t)
                total = total + jnp.where(column == g * (strip - 1), extra, 0.0)
                begin = (t * TH + h) * TW + g * strip
                out_ref[begin : begin + strip] = jnp.where(t < live, total, 0.0).astype(BF16)

    all_metas().wait_send()
    some_rows(0, 1, count - 1).wait_send()

    for e, (down, right) in enumerate(EDGES):
        @pl.when(exists(down, right))
        def _():
            halo_copy(e).wait_send()


def on_device(
    seq_rows, plan_owner, plan_slot, live_frames, norm_gain, norm_bias, conv_weight, conv_bias
):
    rows, channels = seq_rows.shape
    out_width = conv_bias.shape[0]
    tiles = lax.axis_size("tile")
    clips = lax.axis_size("clip")
    count = tiles * clips
    cap = -(-(3 * (rows // count) // 2) // 16) * 16
    joint = joint_of(count, cap)
    dma = pltpu.SemaphoreType.DMA
    decoded = pl.pallas_call(
        functools.partial(decode_kernel, tiles, clips, cap),
        out_shape=pltpu.VMEM((rows, out_width), BF16),
        in_specs=[pl.BlockSpec(memory_space=pltpu.HBM)] * 8,
        out_specs=pl.BlockSpec(memory_space=pltpu.VMEM),
        scratch_shapes=[
            pltpu.SMEM((clips,), jnp.int32),
            pltpu.VMEM((1, rows), jnp.int32),
            pltpu.VMEM((1, rows), jnp.int32),
            pltpu.VMEM((rows, channels), BF16),
            pltpu.VMEM((1, channels), F32),
            pltpu.VMEM((1, channels), F32),
            pltpu.VMEM((1, out_width), F32),
            pltpu.VMEM((3, 3 * channels, 3 * out_width), BF16),
            pltpu.VMEM((count, cap, channels), BF16),
            pltpu.VMEM((count, cap, channels), BF16),
            pltpu.VMEM((count, 1, LANES), F32),
            pltpu.VMEM((count, 1, LANES), F32),
            pltpu.VMEM((count // joint, 1, joint * cap), jnp.int32),
            pltpu.VMEM((rows + EDGE, channels), BF16),
            pltpu.VMEM((LT, TH + 2, TW, 3 * channels), BF16),
            pltpu.VMEM((LT, 2 * TH, 3 * channels), BF16),
            pltpu.VMEM((EDGE, channels), BF16),
            pltpu.VMEM((EDGE, channels), BF16),
            pltpu.VMEM((2, LT * TW, out_width), BF16),
            pltpu.VMEM((2, LT * TW, out_width), BF16),
            pltpu.VMEM((4, 2 * LT, out_width // 2), F32),
            pltpu.VMEM((4, 2 * LT, out_width // 2), F32),
            pltpu.VMEM((LT, PLANE, out_width), F32),
            dma((7,)),
            dma,
            dma,
            dma((count // joint,)),
            dma,
            dma,
            dma((8,)),
            dma((8,)),
        ],
        compiler_params=pltpu.CompilerParams(
            collective_id=0, has_side_effects=True, vmem_limit_bytes=56 << 20
        ),
        name="decode",
    )(
        live_frames,
        plan_owner.reshape(1, rows),
        plan_slot.reshape(1, rows),
        seq_rows,
        norm_gain.reshape(1, channels),
        norm_bias.reshape(1, channels),
        conv_bias.reshape(1, out_width),
        conv_weight.transpose(0, 1, 3, 2, 4).reshape(9, 3 * channels, out_width),
    )

    def finish(held_ref, result_ref, done):
        copy = pltpu.make_async_copy(held_ref, result_ref, done)
        copy.start()
        copy.wait()

    decoded = pl.pallas_call(
        finish,
        out_shape=jax.ShapeDtypeStruct((rows, out_width), BF16),
        in_specs=[pl.BlockSpec(memory_space=pltpu.VMEM)],
        out_specs=pl.BlockSpec(memory_space=pltpu.HBM),
        scratch_shapes=[dma],
        name="finish",
    )(pltpu.with_memory_space_constraint(decoded, pltpu.VMEM))
    return decoded.reshape(1, 1, LT, TH, TW, out_width)


def solution(mesh):
    return jax.shard_map(
        on_device,
        mesh=mesh,
        in_specs=(
            P(("tile", "clip"), None),
            P(("tile", "clip")),
            P(("tile", "clip")),
            P(),
            P(),
            P(),
            P(),
            P(),
        ),
        out_specs=P("clip", "tile", None, None, None, None),
        check_vma=False,
    )
```

```python
import functools

import jax
import jax.numpy as jnp
from jax import lax
from jax.experimental import pallas as pl
from jax.experimental.pallas import tpu as pltpu
from jax.sharding import PartitionSpec as P

GROUPS = 32
LT = 4
TH = 8
TW = 32
GW = 4
PLANE = TH * TW
LANES = 128
STAT = 64
EDGE = 2 * LT * TH
EPSILON = 1e-06
HIGHEST = lax.Precision.HIGHEST
F32 = jnp.float32
BF16 = jnp.bfloat16
NT = (((1,), (1,)), ((), ()))
MESH = pl.DeviceIdType.MESH
EDGES = ((0, 1), (0, -1), (1, 0), (-1, 0), (1, 1), (1, -1), (-1, 1), (-1, -1))


def iota(shape, axis):
    return lax.broadcasted_iota(jnp.int32, shape, axis)


def bits(n):
    return n.bit_length() - 1


def dot(a, b, **kw):
    return jnp.dot(a, b, preferred_element_type=F32, **kw)


def joint_of(count, cap):
    joint = max(1, min(count // 4, 128 // cap))
    while (count // 4) % joint:
        joint -= 1
    return joint


def decode_kernel(
    tiles,
    clips,
    cap,
    live_hbm,
    owner_hbm,
    slot_hbm,
    rows_hbm,
    gain_hbm,
    bias_hbm,
    out_bias_hbm,
    weight_hbm,
    out_ref,
    live_ref,
    owner_ref,
    slot_ref,
    rows_ref,
    gain_ref,
    bias_ref,
    out_bias_ref,
    weight_ref,
    send_rows,
    recv_rows,
    send_meta,
    recv_meta,
    slots_ref,
    placed_ref,
    volume,
    side,
    edge_out,
    edge_in,
    face_out,
    face_in,
    corner_out,
    corner_in,
    summed,
    loaded,
    weight_loaded,
    row_sent,
    row_got,
    meta_sent,
    meta_got,
    halo_sent,
    halo_got,
):
    loads = [
        pltpu.make_async_copy(source, target, loaded.at[i])
        for i, (source, target) in enumerate(
            (
                (owner_hbm, owner_ref),
                (slot_hbm, slot_ref),
                (live_hbm, live_ref),
                (rows_hbm, rows_ref),
                (gain_hbm, gain_ref),
                (bias_hbm, bias_ref),
                (out_bias_hbm, out_bias_ref),
            )
        )
    ]
    rows, channels = rows_ref.shape
    out_width = out_bias_ref.shape[1]
    weight_loads = [
        pltpu.make_async_copy(
            weight_hbm.at[a * 3 + b, pl.ds(d * channels, channels)],
            weight_ref.at[b, pl.ds(a * channels, channels), pl.ds(d * out_width, out_width)],
            weight_loaded,
        )
        for a in range(3)
        for b in range(3)
        for d in range(3)
    ]
    count = tiles * clips
    joint = joint_of(count, cap)
    depth = bits(count)
    half = count // 2
    quarter = count // 4
    own = half
    my_tile = lax.axis_index("tile")
    my_clip = lax.axis_index("clip")
    me = my_tile * clips + my_clip
    far = me // half
    odd = (me // quarter) % 2

    signs = [1 - 2 * ((me // (1 << i)) % 2) for i in range(depth)]
    low_bits = bits(clips)

    def other(mask):
        tile, clip = my_tile, my_clip
        for i in range(depth):
            bit = (mask // (1 << i)) % 2
            if isinstance(bit, int) and not bit:
                continue
            if i < low_bits:
                clip = clip + bit * signs[i] * (1 << i)
            else:
                tile = tile + bit * signs[i] * (1 << (i - low_bits))
        return tile, clip

    def mask_of(k):
        crossing = 1 - k // half
        low = k % half
        if isinstance(k, int):
            bit = low // quarter
            swap = bit + (1 - 2 * bit) * crossing * odd
        else:
            swap = (low // quarter + crossing * odd) % 2
        return crossing * half + low % quarter, swap * quarter

    def partner(k):
        mask, extra = mask_of(k)
        tile, clip = other(mask)
        i = depth - 2
        tile = tile + (extra // quarter) * signs[i] * (1 << (i - low_bits))
        return mask + extra, (tile, clip)

    def each(begin, end, step):
        if end - begin <= 32:
            for k in range(begin, end):
                step(k)
        else:
            pl.loop(begin, end)(step)

    def unless(condition, step):
        if isinstance(condition, bool):
            if not condition:
                step()
        else:
            pl.when(jnp.logical_not(condition))(step)

    barrier = pltpu.get_barrier_semaphore()

    def announce(mask):
        pl.semaphore_signal(barrier, inc=1, device_id=other(count - mask), device_id_type=MESH)

    for load in loads[:2]:
        load.start()
    each(1, count, announce)
    for load in loads[2:]:
        load.start()

    for buffer in (edge_in, face_in, corner_in, volume, side):
        buffer[...] = jnp.zeros_like(buffer)
    chunks = rows // LANES
    before = (iota((LANES, 2 * LANES), 0) < iota((LANES, 2 * LANES), 1)).astype(F32).astype(BF16)
    for load in loads[:2]:
        load.wait()
    owner = owner_ref[...]
    slot = slot_ref[...]
    to_clip = owner >> bits(tiles)
    mask = ((owner & (tiles - 1)) * clips + to_clip) ^ me
    crossing = mask >> (depth - 1)
    order = mask ^ half ^ (crossing * (odd * quarter))
    table = (iota((count, rows), 0) == order).astype(F32)
    table16 = table.astype(BF16)
    stacked = jnp.concatenate([table16[:, c * LANES : (c + 1) * LANES] for c in range(chunks)], axis=0)
    counted = dot(stacked, before)
    base = jnp.zeros((count, LANES), F32)
    ranks = []
    for c in range(chunks):
        part = counted[c * count : (c + 1) * count]
        hit = table[:, c * LANES : (c + 1) * LANES]
        ranks.append(jnp.sum((part[:, :LANES] + base) * hit, axis=0, keepdims=True))
        base = base + part[:, LANES:]
    rank = jnp.concatenate(ranks, axis=1).astype(jnp.int32)
    position = order * cap + rank

    label = slot + 1
    by_rank = (iota((LANES, rows), 0) == rank).astype(F32).astype(BF16)
    digits = jnp.concatenate(
        [table * (label >> 5).astype(F32), table * (label & 31).astype(F32)], axis=0
    ).astype(BF16)
    labels = lax.dot_general(digits, by_rank, NT, preferred_element_type=F32)
    labels = labels[:count] * 32.0 + labels[count:]

    for load in loads[2:4]:
        load.wait()
    for load in weight_loads:
        load.start()
    values = rows_ref[...]
    per_group = bits(channels // GROUPS)

    def partial_sums():
        clip_row = iota((8, rows), 0)
        live_limit = jnp.zeros((8, rows), jnp.int32)
        for c in range(clips):
            live_limit = jnp.where(clip_row == c, live_ref[c] * PLANE, live_limit)
        live_row = ((clip_row == to_clip) & (slot < live_limit)).astype(F32).astype(BF16)
        wide = values.astype(F32)
        square = wide * wide
        high = square.astype(BF16)
        low = (square - high.astype(F32)).astype(BF16)
        sum1 = dot(live_row, values)
        sum2 = dot(live_row, high) + dot(live_row, low)
        group = iota((channels, LANES), 0) >> per_group
        lane = iota((channels, LANES), 1)
        partial = dot(sum1, (lane - STAT == group).astype(F32), precision=HIGHEST) + dot(
            sum2, (lane - STAT - GROUPS == group).astype(F32), precision=HIGHEST
        )
        goes = (my_clip ^ iota((count, LANES), 0)) & (clips - 1)
        stats = jnp.zeros((count, LANES), F32)
        for c in range(clips):
            stats = jnp.where(goes == c, partial[c : c + 1], stats)
        return stats

    def row_copy(k):
        mask, device = partner(k)
        return pltpu.make_async_remote_copy(
            src_ref=send_rows.at[k],
            dst_ref=recv_rows.at[mask],
            send_sem=row_sent,
            recv_sem=row_got.at[mask // joint],
            device_id=device,
            device_id_type=MESH,
        )

    def meta_copy(k):
        mask, device = partner(k)
        return pltpu.make_async_remote_copy(
            src_ref=send_meta.at[k],
            dst_ref=recv_meta.at[mask],
            send_sem=meta_sent,
            recv_sem=meta_got,
            device_id=device,
            device_id_type=MESH,
        )

    batch = max(1, min(quarter // 2, 256 // cap))
    while quarter % batch:
        batch -= 1

    def pack(first, size):
        chosen = (iota((size * cap, rows), 0) + first * cap == position).astype(F32).astype(BF16)
        packed = dot(chosen, values).astype(BF16)
        send_rows[first : first + size] = packed.reshape(size, cap, channels)

    def start_rows(begin, end):
        def step(k):
            row_copy(k).start()
            unless(k == 0, lambda: row_copy(half + k).start())

        each(begin, end, step)

    pack(0, batch)
    pack(half, batch)
    pl.semaphore_wait(barrier, count - 1)
    start_rows(0, batch)
    metas = labels + partial_sums()
    for k in range(count):
        send_meta[k] = metas[k : k + 1]
    recv_meta[0] = send_meta[own]
    each(0, count, lambda k: unless(k == own, lambda: meta_copy(k).start()))
    for first, last in ((batch, quarter), (quarter, half)):
        pack(first, last - first)
        pack(half + first, last - first)
        start_rows(first, last)
    recv_rows[0] = send_rows[own]

    def all_metas():
        return pltpu.make_async_remote_copy(
            src_ref=send_meta.at[pl.ds(0, count - 1)],
            dst_ref=recv_meta.at[pl.ds(1, count - 1)],
            send_sem=meta_sent,
            recv_sem=meta_got,
            device_id=other(1),
            device_id_type=MESH,
        )

    def some_rows(q, first, blocks):
        return pltpu.make_async_remote_copy(
            src_ref=send_rows.at[pl.ds(0, blocks)],
            dst_ref=recv_rows.at[pl.ds(first, blocks)],
            send_sem=row_sent,
            recv_sem=row_got.at[q],
            device_id=other(1),
            device_id_type=MESH,
        )

    all_metas().wait_recv()

    width = joint * cap
    groups = count // joint
    metas_in = jnp.concatenate([recv_meta[m] for m in range(count)], axis=0)
    spread_lane = iota((LANES, width), 0)
    spread_col = iota((LANES, width), 1)
    spread = jnp.zeros((LANES, width), F32)
    block_of = jnp.zeros((count, width), jnp.int32)
    for m in range(joint):
        spread = jnp.where((spread_col - m * cap == spread_lane) & (spread_lane < cap), 1.0, spread)
        block_of = jnp.where(iota((count, width), 1) >= m * cap, m, block_of)
    moved = dot(metas_in, spread, precision=HIGHEST)
    source_of = iota((count, width), 0)
    for q in range(groups):
        keep = source_of == block_of + q * joint
        row = jnp.sum(jnp.where(keep, moved, 0.0), axis=0, keepdims=True)
        slots_ref[q] = (row + 0.5).astype(jnp.int32) - 1

    for load in loads[4:]:
        load.wait()
    live = live_ref[my_clip]
    sums_in = jnp.broadcast_to(jnp.sum(metas_in, axis=0, keepdims=True), (8, LANES))
    voxels = jnp.full((8, LANES), live * ((channels // GROUPS) * PLANE * tiles), jnp.int32)
    scaled = sums_in / voxels.astype(F32)
    stat_lane = iota((LANES, channels), 0)
    stat_group = iota((LANES, channels), 1) >> per_group
    mean = dot(scaled, (stat_lane - STAT == stat_group).astype(F32), precision=HIGHEST)
    second = dot(scaled, (stat_lane - STAT - GROUPS == stat_group).astype(F32), precision=HIGHEST)
    scale = lax.rsqrt(second - mean * mean + EPSILON)
    scale = (0.5 * (scale * gain_ref[...]))[0:1]
    mean = mean[0:1]
    bias = 0.5 * bias_ref[...]

    def activate(raw):
        u = (raw.astype(F32) - mean) * scale + bias
        return (u + u * jnp.tanh(u)).astype(BF16)

    edge_row = iota((EDGE, width), 0)
    edge_voxel = edge_row * TW + jnp.where(edge_row < EDGE // 2, TW - 1, -rows)
    voxel = jnp.concatenate([iota((rows, width), 0), edge_voxel], axis=0)

    def gather(q, blocks=joint):
        some_rows(q, q * joint + joint - blocks, blocks).wait_recv()
        return activate(recv_rows[pl.ds(q * joint, joint)].reshape(width, channels))

    def move(targets, q, arrived):
        return dot((targets == slots_ref[q]).astype(F32).astype(BF16), arrived).astype(BF16)

    half_groups = groups // 2
    quarter_groups = groups // 4
    flip = (odd + 1 - far) % 2

    def group_of(p):
        late = p // half_groups
        low = p % half_groups
        swap = (low // quarter_groups + late * flip) % 2
        return late * half_groups + swap * quarter_groups + low % quarter_groups

    placed_ref[...] = move(voxel, 0, gather(0, joint - 1))

    @pl.loop(1, groups - 1)
    def _(p):
        q = group_of(p)
        placed_ref[...] += move(voxel, q, gather(q))

    grid_rows = tiles // GW
    row_tile = my_tile // GW
    column_tile = my_tile % GW

    def exists(down, right):
        row = row_tile + down
        column = column_tile + right
        return (row >= 0) & (row < grid_rows) & (column >= 0) & (column < GW)

    def halo_copy(e):
        down, right = EDGES[e]
        if e < 2:
            part, source_ref, target_ref = pl.ds(e * (EDGE // 2), EDGE // 2), edge_out, edge_in
        elif e < 4:
            part, source_ref, target_ref = e - 2, face_out, face_in
        else:
            part, source_ref, target_ref = e - 4, corner_out, corner_in
        return pltpu.make_async_remote_copy(
            src_ref=source_ref.at[part],
            dst_ref=target_ref.at[part],
            send_sem=halo_sent.at[e],
            recv_sem=halo_got.at[e],
            device_id=(my_tile + down * GW + right, my_clip),
            device_id_type=MESH,
        )

    def send(e):
        @pl.when(exists(*EDGES[e]))
        def _():
            halo_copy(e).start()

    def receive(e):
        down, right = EDGES[e]

        @pl.when(exists(-down, -right))
        def _():
            halo_copy(e).wait_recv()

    pltpu.make_async_copy(weight_ref, weight_ref, weight_loaded).wait()
    final = group_of(groups - 1)
    tile = placed_ref[...] + move(voxel, final, gather(final))
    edge_out[...] = tile[rows:]
    send(0)
    send(1)
    grid = tile[:rows].reshape(LT, TH, TW, channels)
    for a in range(3):
        volume[2 - a :, 1 : TH + 1, :, a * channels : (a + 1) * channels] = grid[: LT - 2 + a]

    def shifted(product, column):
        taps = [product[:, d * out_width : (d + 1) * out_width] for d in range(3)]
        n = product.shape[0]
        after = jnp.where(column == 0, 0.0, pltpu.roll(taps[0], 1, 0))
        ahead = jnp.where(column == TW - 1, 0.0, pltpu.roll(taps[2], n - 1, 0))
        return after + taps[1] + ahead

    lines = LT * TW
    line_column = iota((lines, out_width), 0) & (TW - 1)
    for f in range(2):
        @pl.when(exists(1 - 2 * f, 0))
        def _():
            b, h = (0, TH) if f == 0 else (2, 1)
            outer = dot(volume[:, h].reshape(lines, 3 * channels), weight_ref[b])
            by_frame = outer.reshape(LT, TW, 3 * out_width)
            for g in range(2):
                w, d = (TW - 1, 0) if g == 0 else (0, 2)
                corner = by_frame[:, w, d * out_width : (d + 1) * out_width]
                corner_out[2 * f + g] = jnp.concatenate(
                    [corner[:, : out_width // 2], corner[:, out_width // 2 :]], axis=0
                )
                send(4 + 2 * f + g)
            face_out[f] = shifted(outer, line_column).astype(BF16)
            send(2 + f)

    plane_column = iota((PLANE, out_width), 0) & (TW - 1)

    out_bias = out_bias_ref[...]

    def frame_sum(t):
        skip = max(0, 2 - t) * channels
        product = None
        for b in range(3):
            slab = volume[t, b : b + TH, :, skip:].reshape(PLANE, 3 * channels - skip)
            term = dot(slab, weight_ref[b, skip:])
            product = term if product is None else product + term
        summed[t] = shifted(product, plane_column) + out_bias

    for t in range(LT):
        frame_sum(t)
    receive(0)
    receive(1)
    edges = edge_in[...].astype(F32)
    edges = jnp.concatenate(
        [edges[n * TH : (n + 1) * TH] for t in range(LT) for n in (t, LT + t)], axis=0
    ).astype(BF16)
    edges = edges.reshape(LT, 2 * TH, channels)
    for a in range(3):
        side[2 - a :, :, a * channels : (a + 1) * channels] = edges[: LT - 2 + a]
    from_left = (iota((EDGE, out_width), 0) & TH) == 0
    line = iota((EDGE, out_width), 0) & (TH - 1)
    beside_in = side[...].reshape(EDGE, 3 * channels)
    taps = []
    for b in range(3):
        taps.append(
            jnp.where(
                from_left,
                dot(beside_in, weight_ref[b, :, :out_width]),
                dot(beside_in, weight_ref[b, :, 2 * out_width :]),
            )
        )
    beside = (
        jnp.where(line == 0, 0.0, pltpu.roll(taps[0], 1, 0))
        + taps[1]
        + jnp.where(line == TH - 1, 0.0, pltpu.roll(taps[2], EDGE - 1, 0))
    )
    for e in range(2, 8):
        receive(e)

    strip = TW // 2
    column = iota((strip, out_width), 0)

    def corner_of(i, t):
        return jnp.concatenate([corner_in[i, t : t + 1], corner_in[i, LT + t : LT + t + 1]], axis=1)

    for t in range(LT):
        for h in range(TH):
            for g in range(2):
                n = t * 2 * TH + g * TH + h
                extra = beside[n : n + 1]
                total = summed[t, h * TW + g * strip : h * TW + (g + 1) * strip]
                if h in (0, TH - 1):
                    f = 0 if h == 0 else 1
                    begin = t * TW + g * strip
                    total = total + face_in[f, begin : begin + strip].astype(F32)
                    extra = extra + corner_of(2 * f + g, t)
                total = total + jnp.where(column == g * (strip - 1), extra, 0.0)
                begin = (t * TH + h) * TW + g * strip
                out_ref[begin : begin + strip] = jnp.where(t < live, total, 0.0).astype(BF16)

    all_metas().wait_send()
    some_rows(0, 1, count - 1).wait_send()

    for e, (down, right) in enumerate(EDGES):
        @pl.when(exists(down, right))
        def _():
            halo_copy(e).wait_send()


def on_device(
    seq_rows, plan_owner, plan_slot, live_frames, norm_gain, norm_bias, conv_weight, conv_bias
):
    rows, channels = seq_rows.shape
    out_width = conv_bias.shape[0]
    tiles = lax.axis_size("tile")
    clips = lax.axis_size("clip")
    count = tiles * clips
    cap = -(-(3 * (rows // count) // 2) // 16) * 16
    joint = joint_of(count, cap)
    dma = pltpu.SemaphoreType.DMA
    decoded = pl.pallas_call(
        functools.partial(decode_kernel, tiles, clips, cap),
        out_shape=pltpu.VMEM((rows, out_width), BF16),
        in_specs=[pl.BlockSpec(memory_space=pltpu.HBM)] * 8,
        out_specs=pl.BlockSpec(memory_space=pltpu.VMEM),
        scratch_shapes=[
            pltpu.SMEM((clips,), jnp.int32),
            pltpu.VMEM((1, rows), jnp.int32),
            pltpu.VMEM((1, rows), jnp.int32),
            pltpu.VMEM((rows, channels), BF16),
            pltpu.VMEM((1, channels), F32),
            pltpu.VMEM((1, channels), F32),
            pltpu.VMEM((1, out_width), F32),
            pltpu.VMEM((3, 3 * channels, 3 * out_width), BF16),
            pltpu.VMEM((count, cap, channels), BF16),
            pltpu.VMEM((count, cap, channels), BF16),
            pltpu.VMEM((count, 1, LANES), F32),
            pltpu.VMEM((count, 1, LANES), F32),
            pltpu.VMEM((count // joint, 1, joint * cap), jnp.int32),
            pltpu.VMEM((rows + EDGE, channels), BF16),
            pltpu.VMEM((LT, TH + 2, TW, 3 * channels), BF16),
            pltpu.VMEM((LT, 2 * TH, 3 * channels), BF16),
            pltpu.VMEM((EDGE, channels), BF16),
            pltpu.VMEM((EDGE, channels), BF16),
            pltpu.VMEM((2, LT * TW, out_width), BF16),
            pltpu.VMEM((2, LT * TW, out_width), BF16),
            pltpu.VMEM((4, 2 * LT, out_width // 2), F32),
            pltpu.VMEM((4, 2 * LT, out_width // 2), F32),
            pltpu.VMEM((LT, PLANE, out_width), F32),
            dma((7,)),
            dma,
            dma,
            dma((count // joint,)),
            dma,
            dma,
            dma((8,)),
            dma((8,)),
        ],
        compiler_params=pltpu.CompilerParams(
            collective_id=0, has_side_effects=True, vmem_limit_bytes=56 << 20
        ),
        name="decode",
    )(
        live_frames,
        plan_owner.reshape(1, rows),
        plan_slot.reshape(1, rows),
        seq_rows,
        norm_gain.reshape(1, channels),
        norm_bias.reshape(1, channels),
        conv_bias.reshape(1, out_width),
        conv_weight.transpose(0, 1, 3, 2, 4).reshape(9, 3 * channels, out_width),
    )

    def finish(held_ref, result_ref, done):
        copy = pltpu.make_async_copy(held_ref, result_ref, done)
        copy.start()
        copy.wait()

    decoded = pl.pallas_call(
        finish,
        out_shape=jax.ShapeDtypeStruct((rows, out_width), BF16),
        in_specs=[pl.BlockSpec(memory_space=pltpu.VMEM)],
        out_specs=pl.BlockSpec(memory_space=pltpu.HBM),
        scratch_shapes=[dma],
        name="finish",
    )(pltpu.with_memory_space_constraint(decoded, pltpu.VMEM))
    return decoded.reshape(1, 1, LT, TH, TW, out_width)


def solution(mesh):
    return jax.shard_map(
        on_device,
        mesh=mesh,
        in_specs=(
            P(("tile", "clip"), None),
            P(("tile", "clip")),
            P(("tile", "clip")),
            P(),
            P(),
            P(),
            P(),
            P(),
        ),
        out_specs=P("clip", "tile", None, None, None, None),
        check_vma=False,
    )
```

```python
import functools

import jax
import jax.numpy as jnp
from jax import lax
from jax.experimental import pallas as pl
from jax.experimental.pallas import tpu as pltpu
from jax.sharding import PartitionSpec as P

GROUPS = 32
LT = 4
TH = 8
TW = 32
GW = 4
PLANE = TH * TW
LANES = 128
STAT = 64
EDGE = 2 * LT * TH
EPSILON = 1e-06
HIGHEST = lax.Precision.HIGHEST
F32 = jnp.float32
BF16 = jnp.bfloat16
NT = (((1,), (1,)), ((), ()))
MESH = pl.DeviceIdType.MESH
EDGES = ((0, 1), (0, -1), (1, 0), (-1, 0), (1, 1), (1, -1), (-1, 1), (-1, -1))


def iota(shape, axis):
    return lax.broadcasted_iota(jnp.int32, shape, axis)


def bits(n):
    return n.bit_length() - 1


def dot(a, b, **kw):
    return jnp.dot(a, b, preferred_element_type=F32, **kw)


def joint_of(count, cap):
    joint = max(1, min(count // 4, 128 // cap))
    while (count // 4) % joint:
        joint -= 1
    return joint


def decode_kernel(
    tiles,
    clips,
    cap,
    live_hbm,
    owner_hbm,
    slot_hbm,
    rows_hbm,
    gain_hbm,
    bias_hbm,
    out_bias_hbm,
    weight_hbm,
    out_ref,
    live_ref,
    owner_ref,
    slot_ref,
    rows_ref,
    gain_ref,
    bias_ref,
    out_bias_ref,
    weight_ref,
    send_rows,
    recv_rows,
    send_meta,
    recv_meta,
    slots_ref,
    placed_ref,
    volume,
    side,
    edge_out,
    edge_in,
    face_out,
    face_in,
    corner_out,
    corner_in,
    summed,
    loaded,
    weight_loaded,
    row_sent,
    row_got,
    meta_sent,
    meta_got,
    halo_sent,
    halo_got,
):
    loads = [
        pltpu.make_async_copy(source, target, loaded.at[i])
        for i, (source, target) in enumerate(
            (
                (owner_hbm, owner_ref),
                (slot_hbm, slot_ref),
                (live_hbm, live_ref),
                (rows_hbm, rows_ref),
                (gain_hbm, gain_ref),
                (bias_hbm, bias_ref),
                (out_bias_hbm, out_bias_ref),
            )
        )
    ]
    rows, channels = rows_ref.shape
    out_width = out_bias_ref.shape[1]
    weight_loads = [
        pltpu.make_async_copy(
            weight_hbm.at[a * 3 + b, pl.ds(d * channels, channels)],
            weight_ref.at[b, pl.ds(a * channels, channels), pl.ds(d * out_width, out_width)],
            weight_loaded,
        )
        for a in range(3)
        for b in range(3)
        for d in range(3)
    ]
    count = tiles * clips
    joint = joint_of(count, cap)
    depth = bits(count)
    half = count // 2
    quarter = count // 4
    own = half
    my_tile = lax.axis_index("tile")
    my_clip = lax.axis_index("clip")
    me = my_tile * clips + my_clip
    far = me // half
    odd = (me // quarter) % 2

    signs = [1 - 2 * ((me // (1 << i)) % 2) for i in range(depth)]
    low_bits = bits(clips)

    def other(mask):
        tile, clip = my_tile, my_clip
        for i in range(depth):
            bit = (mask // (1 << i)) % 2
            if isinstance(bit, int) and not bit:
                continue
            if i < low_bits:
                clip = clip + bit * signs[i] * (1 << i)
            else:
                tile = tile + bit * signs[i] * (1 << (i - low_bits))
        return tile, clip

    def mask_of(k):
        crossing = 1 - k // half
        low = k % half
        if isinstance(k, int):
            bit = low // quarter
            swap = bit + (1 - 2 * bit) * crossing * odd
        else:
            swap = (low // quarter + crossing * odd) % 2
        return crossing * half + low % quarter, swap * quarter

    def partner(k):
        mask, extra = mask_of(k)
        tile, clip = other(mask)
        i = depth - 2
        tile = tile + (extra // quarter) * signs[i] * (1 << (i - low_bits))
        return mask + extra, (tile, clip)

    def each(begin, end, step):
        if end - begin <= 32:
            for k in range(begin, end):
                step(k)
        else:
            pl.loop(begin, end)(step)

    def unless(condition, step):
        if isinstance(condition, bool):
            if not condition:
                step()
        else:
            pl.when(jnp.logical_not(condition))(step)

    barrier = pltpu.get_barrier_semaphore()

    def announce(mask):
        pl.semaphore_signal(barrier, inc=1, device_id=other(count - mask), device_id_type=MESH)

    for load in loads[:2]:
        load.start()
    each(1, count, announce)
    for load in loads[2:]:
        load.start()

    for buffer in (edge_in, face_in, corner_in, volume, side):
        buffer[...] = jnp.zeros_like(buffer)
    chunks = rows // LANES
    before = (iota((LANES, 2 * LANES), 0) < iota((LANES, 2 * LANES), 1)).astype(F32).astype(BF16)
    for load in loads[:2]:
        load.wait()
    owner = owner_ref[...]
    slot = slot_ref[...]
    to_clip = owner >> bits(tiles)
    mask = ((owner & (tiles - 1)) * clips + to_clip) ^ me
    crossing = mask >> (depth - 1)
    order = mask ^ half ^ (crossing * (odd * quarter))
    table = (iota((count, rows), 0) == order).astype(F32)
    table16 = table.astype(BF16)
    stacked = jnp.concatenate([table16[:, c * LANES : (c + 1) * LANES] for c in range(chunks)], axis=0)
    counted = dot(stacked, before)
    base = jnp.zeros((count, LANES), F32)
    ranks = []
    for c in range(chunks):
        part = counted[c * count : (c + 1) * count]
        hit = table[:, c * LANES : (c + 1) * LANES]
        ranks.append(jnp.sum((part[:, :LANES] + base) * hit, axis=0, keepdims=True))
        base = base + part[:, LANES:]
    rank = jnp.concatenate(ranks, axis=1).astype(jnp.int32)
    position = order * cap + rank

    label = slot + 1
    by_rank = (iota((LANES, rows), 0) == rank).astype(F32).astype(BF16)
    digits = jnp.concatenate(
        [table * (label >> 5).astype(F32), table * (label & 31).astype(F32)], axis=0
    ).astype(BF16)
    labels = lax.dot_general(digits, by_rank, NT, preferred_element_type=F32)
    labels = labels[:count] * 32.0 + labels[count:]

    for load in loads[2:4]:
        load.wait()
    for load in weight_loads:
        load.start()
    values = rows_ref[...]
    per_group = bits(channels // GROUPS)

    def partial_sums():
        clip_row = iota((8, rows), 0)
        live_limit = jnp.zeros((8, rows), jnp.int32)
        for c in range(clips):
            live_limit = jnp.where(clip_row == c, live_ref[c] * PLANE, live_limit)
        live_row = ((clip_row == to_clip) & (slot < live_limit)).astype(F32).astype(BF16)
        wide = values.astype(F32)
        square = wide * wide
        high = square.astype(BF16)
        low = (square - high.astype(F32)).astype(BF16)
        sum1 = dot(live_row, values)
        sum2 = dot(live_row, high) + dot(live_row, low)
        group = iota((channels, LANES), 0) >> per_group
        lane = iota((channels, LANES), 1)
        partial = dot(sum1, (lane - STAT == group).astype(F32), precision=HIGHEST) + dot(
            sum2, (lane - STAT - GROUPS == group).astype(F32), precision=HIGHEST
        )
        goes = (my_clip ^ iota((count, LANES), 0)) & (clips - 1)
        stats = jnp.zeros((count, LANES), F32)
        for c in range(clips):
            stats = jnp.where(goes == c, partial[c : c + 1], stats)
        return stats

    def row_copy(k):
        mask, device = partner(k)
        return pltpu.make_async_remote_copy(
            src_ref=send_rows.at[k],
            dst_ref=recv_rows.at[mask],
            send_sem=row_sent,
            recv_sem=row_got.at[mask // joint],
            device_id=device,
            device_id_type=MESH,
        )

    def meta_copy(k):
        mask, device = partner(k)
        return pltpu.make_async_remote_copy(
            src_ref=send_meta.at[k],
            dst_ref=recv_meta.at[mask],
            send_sem=meta_sent,
            recv_sem=meta_got,
            device_id=device,
            device_id_type=MESH,
        )

    batch = max(1, min(quarter // 2, 256 // cap))
    while quarter % batch:
        batch -= 1

    def pack(first, size):
        chosen = (iota((size * cap, rows), 0) + first * cap == position).astype(F32).astype(BF16)
        packed = dot(chosen, values).astype(BF16)
        send_rows[first : first + size] = packed.reshape(size, cap, channels)

    def start_rows(begin, end):
        def step(k):
            row_copy(k).start()
            unless(k == 0, lambda: row_copy(half + k).start())

        each(begin, end, step)

    pack(0, batch)
    pack(half, batch)
    pl.semaphore_wait(barrier, count - 1)
    start_rows(0, batch)
    metas = labels + partial_sums()
    for k in range(count):
        send_meta[k] = metas[k : k + 1]
    recv_meta[0] = send_meta[own]
    each(0, count, lambda k: unless(k == own, lambda: meta_copy(k).start()))
    for first, last in ((batch, quarter), (quarter, half)):
        pack(first, last - first)
        pack(half + first, last - first)
        start_rows(first, last)
    recv_rows[0] = send_rows[own]

    def all_metas():
        return pltpu.make_async_remote_copy(
            src_ref=send_meta.at[pl.ds(0, count - 1)],
            dst_ref=recv_meta.at[pl.ds(1, count - 1)],
            send_sem=meta_sent,
            recv_sem=meta_got,
            device_id=other(1),
            device_id_type=MESH,
        )

    def some_rows(q, first, blocks):
        return pltpu.make_async_remote_copy(
            src_ref=send_rows.at[pl.ds(0, blocks)],
            dst_ref=recv_rows.at[pl.ds(first, blocks)],
            send_sem=row_sent,
            recv_sem=row_got.at[q],
            device_id=other(1),
            device_id_type=MESH,
        )

    all_metas().wait_recv()

    width = joint * cap
    groups = count // joint
    metas_in = jnp.concatenate([recv_meta[m] for m in range(count)], axis=0)
    spread_lane = iota((LANES, width), 0)
    spread_col = iota((LANES, width), 1)
    spread = jnp.zeros((LANES, width), F32)
    block_of = jnp.zeros((count, width), jnp.int32)
    for m in range(joint):
        spread = jnp.where((spread_col - m * cap == spread_lane) & (spread_lane < cap), 1.0, spread)
        block_of = jnp.where(iota((count, width), 1) >= m * cap, m, block_of)
    moved = dot(metas_in, spread, precision=HIGHEST)
    source_of = iota((count, width), 0)
    for q in range(groups):
        keep = source_of == block_of + q * joint
        row = jnp.sum(jnp.where(keep, moved, 0.0), axis=0, keepdims=True)
        slots_ref[q] = (row + 0.5).astype(jnp.int32) - 1

    for load in loads[4:]:
        load.wait()
    live = live_ref[my_clip]
    sums_in = jnp.broadcast_to(jnp.sum(metas_in, axis=0, keepdims=True), (8, LANES))
    voxels = jnp.full((8, LANES), live * ((channels // GROUPS) * PLANE * tiles), jnp.int32)
    scaled = sums_in / voxels.astype(F32)
    stat_lane = iota((LANES, channels), 0)
    stat_group = iota((LANES, channels), 1) >> per_group
    mean = dot(scaled, (stat_lane - STAT == stat_group).astype(F32), precision=HIGHEST)
    second = dot(scaled, (stat_lane - STAT - GROUPS == stat_group).astype(F32), precision=HIGHEST)
    scale = lax.rsqrt(second - mean * mean + EPSILON)
    scale = (0.5 * (scale * gain_ref[...]))[0:1]
    mean = mean[0:1]
    bias = 0.5 * bias_ref[...]

    def activate(raw):
        u = (raw.astype(F32) - mean) * scale + bias
        return (u + u * jnp.tanh(u)).astype(BF16)

    edge_row = iota((EDGE, width), 0)
    edge_voxel = edge_row * TW + jnp.where(edge_row < EDGE // 2, TW - 1, -rows)
    voxel = jnp.concatenate([iota((rows, width), 0), edge_voxel], axis=0)

    def gather(q, blocks=joint):
        some_rows(q, q * joint + joint - blocks, blocks).wait_recv()
        return activate(recv_rows[pl.ds(q * joint, joint)].reshape(width, channels))

    def move(targets, q, arrived):
        return dot((targets == slots_ref[q]).astype(F32).astype(BF16), arrived).astype(BF16)

    half_groups = groups // 2
    quarter_groups = groups // 4
    flip = (odd + 1 - far) % 2

    def group_of(p):
        late = p // half_groups
        low = p % half_groups
        swap = (low // quarter_groups + late * flip) % 2
        return late * half_groups + swap * quarter_groups + low % quarter_groups

    placed_ref[...] = move(voxel, 0, gather(0, joint - 1))

    @pl.loop(1, groups - 1)
    def _(p):
        q = group_of(p)
        placed_ref[...] += move(voxel, q, gather(q))

    grid_rows = tiles // GW
    row_tile = my_tile // GW
    column_tile = my_tile % GW

    def exists(down, right):
        row = row_tile + down
        column = column_tile + right
        return (row >= 0) & (row < grid_rows) & (column >= 0) & (column < GW)

    def halo_copy(e):
        down, right = EDGES[e]
        if e < 2:
            part, source_ref, target_ref = pl.ds(e * (EDGE // 2), EDGE // 2), edge_out, edge_in
        elif e < 4:
            part, source_ref, target_ref = e - 2, face_out, face_in
        else:
            part, source_ref, target_ref = e - 4, corner_out, corner_in
        return pltpu.make_async_remote_copy(
            src_ref=source_ref.at[part],
            dst_ref=target_ref.at[part],
            send_sem=halo_sent.at[e],
            recv_sem=halo_got.at[e],
            device_id=(my_tile + down * GW + right, my_clip),
            device_id_type=MESH,
        )

    def send(e):
        @pl.when(exists(*EDGES[e]))
        def _():
            halo_copy(e).start()

    def receive(e):
        down, right = EDGES[e]

        @pl.when(exists(-down, -right))
        def _():
            halo_copy(e).wait_recv()

    pltpu.make_async_copy(weight_ref, weight_ref, weight_loaded).wait()
    final = group_of(groups - 1)
    tile = placed_ref[...] + move(voxel, final, gather(final))
    edge_out[...] = tile[rows:]
    send(0)
    send(1)
    grid = tile[:rows].reshape(LT, TH, TW, channels)
    for a in range(3):
        volume[2 - a :, 1 : TH + 1, :, a * channels : (a + 1) * channels] = grid[: LT - 2 + a]

    def shifted(product, column):
        taps = [product[:, d * out_width : (d + 1) * out_width] for d in range(3)]
        n = product.shape[0]
        after = jnp.where(column == 0, 0.0, pltpu.roll(taps[0], 1, 0))
        ahead = jnp.where(column == TW - 1, 0.0, pltpu.roll(taps[2], n - 1, 0))
        return after + taps[1] + ahead

    lines = LT * TW
    line_column = iota((lines, out_width), 0) & (TW - 1)
    for f in range(2):
        @pl.when(exists(1 - 2 * f, 0))
        def _():
            b, h = (0, TH) if f == 0 else (2, 1)
            outer = dot(volume[:, h].reshape(lines, 3 * channels), weight_ref[b])
            by_frame = outer.reshape(LT, TW, 3 * out_width)
            for g in range(2):
                w, d = (TW - 1, 0) if g == 0 else (0, 2)
                corner = by_frame[:, w, d * out_width : (d + 1) * out_width]
                corner_out[2 * f + g] = jnp.concatenate(
                    [corner[:, : out_width // 2], corner[:, out_width // 2 :]], axis=0
                )
                send(4 + 2 * f + g)
            face_out[f] = shifted(outer, line_column).astype(BF16)
            send(2 + f)

    plane_column = iota((PLANE, out_width), 0) & (TW - 1)

    out_bias = out_bias_ref[...]

    def frame_sum(t):
        skip = max(0, 2 - t) * channels
        product = None
        for b in range(3):
            slab = volume[t, b : b + TH, :, skip:].reshape(PLANE, 3 * channels - skip)
            term = dot(slab, weight_ref[b, skip:])
            product = term if product is None else product + term
        summed[t] = shifted(product, plane_column) + out_bias

    for t in range(LT):
        frame_sum(t)
    receive(0)
    receive(1)
    edges = edge_in[...].astype(F32)
    edges = jnp.concatenate(
        [edges[n * TH : (n + 1) * TH] for t in range(LT) for n in (t, LT + t)], axis=0
    ).astype(BF16)
    edges = edges.reshape(LT, 2 * TH, channels)
    for a in range(3):
        side[2 - a :, :, a * channels : (a + 1) * channels] = edges[: LT - 2 + a]
    from_left = (iota((EDGE, out_width), 0) & TH) == 0
    line = iota((EDGE, out_width), 0) & (TH - 1)
    beside_in = side[...].reshape(EDGE, 3 * channels)
    taps = []
    for b in range(3):
        taps.append(
            jnp.where(
                from_left,
                dot(beside_in, weight_ref[b, :, :out_width]),
                dot(beside_in, weight_ref[b, :, 2 * out_width :]),
            )
        )
    beside = (
        jnp.where(line == 0, 0.0, pltpu.roll(taps[0], 1, 0))
        + taps[1]
        + jnp.where(line == TH - 1, 0.0, pltpu.roll(taps[2], EDGE - 1, 0))
    )

    strip = TW // 2
    column = iota((strip, out_width), 0)

    def corner_of(i, t):
        return jnp.concatenate([corner_in[i, t : t + 1], corner_in[i, LT + t : LT + t + 1]], axis=1)

    def assemble(lines):
        for t, h in [(t, h) for t in range(LT) for h in lines]:
            for g in range(2):
                n = t * 2 * TH + g * TH + h
                extra = beside[n : n + 1]
                total = summed[t, h * TW + g * strip : h * TW + (g + 1) * strip]
                if h in (0, TH - 1):
                    f = 0 if h == 0 else 1
                    begin = t * TW + g * strip
                    total = total + face_in[f, begin : begin + strip].astype(F32)
                    extra = extra + corner_of(2 * f + g, t)
                total = total + jnp.where(column == g * (strip - 1), extra, 0.0)
                begin = (t * TH + h) * TW + g * strip
                out_ref[begin : begin + strip] = jnp.where(t < live, total, 0.0).astype(BF16)

    assemble(range(1, TH - 1))
    all_metas().wait_send()
    some_rows(0, 1, count - 1).wait_send()
    for e in range(2, 8):
        receive(e)
    assemble((0, TH - 1))

    for e, (down, right) in enumerate(EDGES):
        @pl.when(exists(down, right))
        def _():
            halo_copy(e).wait_send()


def on_device(
    seq_rows, plan_owner, plan_slot, live_frames, norm_gain, norm_bias, conv_weight, conv_bias
):
    rows, channels = seq_rows.shape
    out_width = conv_bias.shape[0]
    tiles = lax.axis_size("tile")
    clips = lax.axis_size("clip")
    count = tiles * clips
    cap = -(-(3 * (rows // count) // 2) // 16) * 16
    joint = joint_of(count, cap)
    dma = pltpu.SemaphoreType.DMA
    decoded = pl.pallas_call(
        functools.partial(decode_kernel, tiles, clips, cap),
        out_shape=pltpu.VMEM((rows, out_width), BF16),
        in_specs=[pl.BlockSpec(memory_space=pltpu.HBM)] * 8,
        out_specs=pl.BlockSpec(memory_space=pltpu.VMEM),
        scratch_shapes=[
            pltpu.SMEM((clips,), jnp.int32),
            pltpu.VMEM((1, rows), jnp.int32),
            pltpu.VMEM((1, rows), jnp.int32),
            pltpu.VMEM((rows, channels), BF16),
            pltpu.VMEM((1, channels), F32),
            pltpu.VMEM((1, channels), F32),
            pltpu.VMEM((1, out_width), F32),
            pltpu.VMEM((3, 3 * channels, 3 * out_width), BF16),
            pltpu.VMEM((count, cap, channels), BF16),
            pltpu.VMEM((count, cap, channels), BF16),
            pltpu.VMEM((count, 1, LANES), F32),
            pltpu.VMEM((count, 1, LANES), F32),
            pltpu.VMEM((count // joint, 1, joint * cap), jnp.int32),
            pltpu.VMEM((rows + EDGE, channels), BF16),
            pltpu.VMEM((LT, TH + 2, TW, 3 * channels), BF16),
            pltpu.VMEM((LT, 2 * TH, 3 * channels), BF16),
            pltpu.VMEM((EDGE, channels), BF16),
            pltpu.VMEM((EDGE, channels), BF16),
            pltpu.VMEM((2, LT * TW, out_width), BF16),
            pltpu.VMEM((2, LT * TW, out_width), BF16),
            pltpu.VMEM((4, 2 * LT, out_width // 2), F32),
            pltpu.VMEM((4, 2 * LT, out_width // 2), F32),
            pltpu.VMEM((LT, PLANE, out_width), F32),
            dma((7,)),
            dma,
            dma,
            dma((count // joint,)),
            dma,
            dma,
            dma((8,)),
            dma((8,)),
        ],
        compiler_params=pltpu.CompilerParams(
            collective_id=0, has_side_effects=True, vmem_limit_bytes=56 << 20
        ),
        name="decode",
    )(
        live_frames,
        plan_owner.reshape(1, rows),
        plan_slot.reshape(1, rows),
        seq_rows,
        norm_gain.reshape(1, channels),
        norm_bias.reshape(1, channels),
        conv_bias.reshape(1, out_width),
        conv_weight.transpose(0, 1, 3, 2, 4).reshape(9, 3 * channels, out_width),
    )

    def finish(held_ref, result_ref, done):
        copy = pltpu.make_async_copy(held_ref, result_ref, done)
        copy.start()
        copy.wait()

    decoded = pl.pallas_call(
        finish,
        out_shape=jax.ShapeDtypeStruct((rows, out_width), BF16),
        in_specs=[pl.BlockSpec(memory_space=pltpu.VMEM)],
        out_specs=pl.BlockSpec(memory_space=pltpu.HBM),
        scratch_shapes=[dma],
        name="finish",
    )(pltpu.with_memory_space_constraint(decoded, pltpu.VMEM))
    return decoded.reshape(1, 1, LT, TH, TW, out_width)


def solution(mesh):
    return jax.shard_map(
        on_device,
        mesh=mesh,
        in_specs=(
            P(("tile", "clip"), None),
            P(("tile", "clip")),
            P(("tile", "clip")),
            P(),
            P(),
            P(),
            P(),
            P(),
        ),
        out_specs=P("clip", "tile", None, None, None, None),
        check_vma=False,
    )
```

```python
import functools

import jax
import jax.numpy as jnp
from jax import lax
from jax.experimental import pallas as pl
from jax.experimental.pallas import tpu as pltpu
from jax.sharding import PartitionSpec as P

GROUPS = 32
LT = 4
TH = 8
TW = 32
GW = 4
PLANE = TH * TW
LANES = 128
STAT = 64
EDGE = 2 * LT * TH
EPSILON = 1e-06
HIGHEST = lax.Precision.HIGHEST
F32 = jnp.float32
BF16 = jnp.bfloat16
NT = (((1,), (1,)), ((), ()))
MESH = pl.DeviceIdType.MESH
EDGES = ((0, 1), (0, -1), (1, 0), (-1, 0), (1, 1), (1, -1), (-1, 1), (-1, -1))


def iota(shape, axis):
    return lax.broadcasted_iota(jnp.int32, shape, axis)


def bits(n):
    return n.bit_length() - 1


def dot(a, b, **kw):
    return jnp.dot(a, b, preferred_element_type=F32, **kw)


def joint_of(count, cap):
    joint = max(1, min(count // 4, 128 // cap))
    while (count // 4) % joint:
        joint -= 1
    return joint


def decode_kernel(
    tiles,
    clips,
    cap,
    live_hbm,
    owner_hbm,
    slot_hbm,
    rows_hbm,
    gain_hbm,
    bias_hbm,
    out_bias_hbm,
    weight_hbm,
    out_ref,
    live_ref,
    owner_ref,
    slot_ref,
    rows_ref,
    gain_ref,
    bias_ref,
    out_bias_ref,
    weight_ref,
    send_rows,
    recv_rows,
    send_meta,
    recv_meta,
    slots_ref,
    placed_ref,
    volume,
    side,
    edge_out,
    edge_in,
    face_out,
    face_in,
    corner_out,
    corner_in,
    summed,
    loaded,
    weight_loaded,
    row_sent,
    row_got,
    meta_sent,
    meta_got,
    halo_sent,
    halo_got,
):
    loads = [
        pltpu.make_async_copy(source, target, loaded.at[i])
        for i, (source, target) in enumerate(
            (
                (owner_hbm, owner_ref),
                (slot_hbm, slot_ref),
                (live_hbm, live_ref),
                (rows_hbm, rows_ref),
                (gain_hbm, gain_ref),
                (bias_hbm, bias_ref),
                (out_bias_hbm, out_bias_ref),
            )
        )
    ]
    rows, channels = rows_ref.shape
    out_width = out_bias_ref.shape[1]
    weight_loads = [
        pltpu.make_async_copy(
            weight_hbm.at[a * 3 + b, pl.ds(d * channels, channels)],
            weight_ref.at[b, pl.ds(a * channels, channels), pl.ds(d * out_width, out_width)],
            weight_loaded,
        )
        for a in range(3)
        for b in range(3)
        for d in range(3)
    ]
    count = tiles * clips
    joint = joint_of(count, cap)
    depth = bits(count)
    half = count // 2
    quarter = count // 4
    own = half
    my_tile = lax.axis_index("tile")
    my_clip = lax.axis_index("clip")
    me = my_tile * clips + my_clip
    far = me // half
    odd = (me // quarter) % 2

    signs = [1 - 2 * ((me // (1 << i)) % 2) for i in range(depth)]
    low_bits = bits(clips)

    def other(mask):
        tile, clip = my_tile, my_clip
        for i in range(depth):
            bit = (mask // (1 << i)) % 2
            if isinstance(bit, int) and not bit:
                continue
            if i < low_bits:
                clip = clip + bit * signs[i] * (1 << i)
            else:
                tile = tile + bit * signs[i] * (1 << (i - low_bits))
        return tile, clip

    def mask_of(k):
        crossing = 1 - k // half
        low = k % half
        if isinstance(k, int):
            bit = low // quarter
            swap = bit + (1 - 2 * bit) * crossing * odd
        else:
            swap = (low // quarter + crossing * odd) % 2
        return crossing * half + low % quarter, swap * quarter

    def partner(k):
        mask, extra = mask_of(k)
        tile, clip = other(mask)
        i = depth - 2
        tile = tile + (extra // quarter) * signs[i] * (1 << (i - low_bits))
        return mask + extra, (tile, clip)

    def each(begin, end, step):
        if end - begin <= 32:
            for k in range(begin, end):
                step(k)
        else:
            pl.loop(begin, end)(step)

    def unless(condition, step):
        if isinstance(condition, bool):
            if not condition:
                step()
        else:
            pl.when(jnp.logical_not(condition))(step)

    barrier = pltpu.get_barrier_semaphore()

    def announce(mask):
        pl.semaphore_signal(barrier, inc=1, device_id=other(count - mask), device_id_type=MESH)

    for load in loads[:2]:
        load.start()
    each(1, count, announce)
    for load in loads[2:]:
        load.start()

    for buffer in (edge_in, face_in, corner_in, volume, side):
        buffer[...] = jnp.zeros_like(buffer)
    chunks = rows // LANES
    before = (iota((LANES, 2 * LANES), 0) < iota((LANES, 2 * LANES), 1)).astype(F32).astype(BF16)
    for load in loads[:2]:
        load.wait()
    owner = owner_ref[...]
    slot = slot_ref[...]
    to_clip = owner >> bits(tiles)
    mask = ((owner & (tiles - 1)) * clips + to_clip) ^ me
    crossing = mask >> (depth - 1)
    order = mask ^ half ^ (crossing * (odd * quarter))
    table = (iota((count, rows), 0) == order).astype(F32)
    table16 = table.astype(BF16)
    stacked = jnp.concatenate([table16[:, c * LANES : (c + 1) * LANES] for c in range(chunks)], axis=0)
    counted = dot(stacked, before)
    base = jnp.zeros((count, LANES), F32)
    ranks = []
    for c in range(chunks):
        part = counted[c * count : (c + 1) * count]
        hit = table[:, c * LANES : (c + 1) * LANES]
        ranks.append(jnp.sum((part[:, :LANES] + base) * hit, axis=0, keepdims=True))
        base = base + part[:, LANES:]
    rank = jnp.concatenate(ranks, axis=1).astype(jnp.int32)
    position = order * cap + rank

    label = slot + 1
    by_rank = (iota((LANES, rows), 0) == rank).astype(F32).astype(BF16)
    digits = jnp.concatenate(
        [table * (label >> 5).astype(F32), table * (label & 31).astype(F32)], axis=0
    ).astype(BF16)
    labels = lax.dot_general(digits, by_rank, NT, preferred_element_type=F32)
    labels = labels[:count] * 32.0 + labels[count:]

    for load in loads[2:4]:
        load.wait()
    for load in weight_loads:
        load.start()
    values = rows_ref[...]
    per_group = bits(channels // GROUPS)

    def partial_sums():
        clip_row = iota((8, rows), 0)
        live_limit = jnp.zeros((8, rows), jnp.int32)
        for c in range(clips):
            live_limit = jnp.where(clip_row == c, live_ref[c] * PLANE, live_limit)
        live_row = ((clip_row == to_clip) & (slot < live_limit)).astype(F32).astype(BF16)
        wide = values.astype(F32)
        square = wide * wide
        high = square.astype(BF16)
        low = (square - high.astype(F32)).astype(BF16)
        sum1 = dot(live_row, values)
        sum2 = dot(live_row, high) + dot(live_row, low)
        group = iota((channels, LANES), 0) >> per_group
        lane = iota((channels, LANES), 1)
        partial = dot(sum1, (lane - STAT == group).astype(F32), precision=HIGHEST) + dot(
            sum2, (lane - STAT - GROUPS == group).astype(F32), precision=HIGHEST
        )
        goes = (my_clip ^ iota((count, LANES), 0)) & (clips - 1)
        stats = jnp.zeros((count, LANES), F32)
        for c in range(clips):
            stats = jnp.where(goes == c, partial[c : c + 1], stats)
        return stats

    def row_copy(k):
        mask, device = partner(k)
        return pltpu.make_async_remote_copy(
            src_ref=send_rows.at[k],
            dst_ref=recv_rows.at[mask],
            send_sem=row_sent,
            recv_sem=row_got.at[mask // joint],
            device_id=device,
            device_id_type=MESH,
        )

    def meta_copy(k):
        mask, device = partner(k)
        return pltpu.make_async_remote_copy(
            src_ref=send_meta.at[k],
            dst_ref=recv_meta.at[mask],
            send_sem=meta_sent,
            recv_sem=meta_got,
            device_id=device,
            device_id_type=MESH,
        )

    batch = max(1, min(quarter // 2, 256 // cap))
    while quarter % batch:
        batch -= 1

    def pack(first, size):
        chosen = (iota((size * cap, rows), 0) + first * cap == position).astype(F32).astype(BF16)
        packed = dot(chosen, values).astype(BF16)
        send_rows[first : first + size] = packed.reshape(size, cap, channels)

    def start_rows(begin, end):
        def step(k):
            row_copy(k).start()
            unless(k == 0, lambda: row_copy(half + k).start())

        each(begin, end, step)

    pack(0, batch)
    pack(half, batch)
    pl.semaphore_wait(barrier, count - 1)
    start_rows(0, batch)
    metas = labels + partial_sums()
    for k in range(count):
        send_meta[k] = metas[k : k + 1]
    recv_meta[0] = send_meta[own]
    each(0, count, lambda k: unless(k == own, lambda: meta_copy(k).start()))
    for first, last in ((batch, quarter), (quarter, half)):
        pack(first, last - first)
        pack(half + first, last - first)
        start_rows(first, last)
    recv_rows[0] = send_rows[own]

    def all_metas():
        return pltpu.make_async_remote_copy(
            src_ref=send_meta.at[pl.ds(0, count - 1)],
            dst_ref=recv_meta.at[pl.ds(1, count - 1)],
            send_sem=meta_sent,
            recv_sem=meta_got,
            device_id=other(1),
            device_id_type=MESH,
        )

    def some_rows(q, first, blocks):
        return pltpu.make_async_remote_copy(
            src_ref=send_rows.at[pl.ds(0, blocks)],
            dst_ref=recv_rows.at[pl.ds(first, blocks)],
            send_sem=row_sent,
            recv_sem=row_got.at[q],
            device_id=other(1),
            device_id_type=MESH,
        )

    all_metas().wait_recv()

    width = joint * cap
    groups = count // joint
    metas_in = jnp.concatenate([recv_meta[m] for m in range(count)], axis=0)
    spread_lane = iota((LANES, width), 0)
    spread_col = iota((LANES, width), 1)
    spread = jnp.zeros((LANES, width), F32)
    block_of = jnp.zeros((count, width), jnp.int32)
    for m in range(joint):
        spread = jnp.where((spread_col - m * cap == spread_lane) & (spread_lane < cap), 1.0, spread)
        block_of = jnp.where(iota((count, width), 1) >= m * cap, m, block_of)
    moved = dot(metas_in, spread, precision=HIGHEST)
    source_of = iota((count, width), 0)
    for q in range(groups):
        keep = source_of == block_of + q * joint
        row = jnp.sum(jnp.where(keep, moved, 0.0), axis=0, keepdims=True)
        slots_ref[q] = (row + 0.5).astype(jnp.int32) - 1

    for load in loads[4:]:
        load.wait()
    live = live_ref[my_clip]
    sums_in = jnp.broadcast_to(jnp.sum(metas_in, axis=0, keepdims=True), (8, LANES))
    voxels = jnp.full((8, LANES), live * ((channels // GROUPS) * PLANE * tiles), jnp.int32)
    scaled = sums_in / voxels.astype(F32)
    stat_lane = iota((LANES, channels), 0)
    stat_group = iota((LANES, channels), 1) >> per_group
    mean = dot(scaled, (stat_lane - STAT == stat_group).astype(F32), precision=HIGHEST)
    second = dot(scaled, (stat_lane - STAT - GROUPS == stat_group).astype(F32), precision=HIGHEST)
    scale = lax.rsqrt(second - mean * mean + EPSILON)
    scale = (0.5 * (scale * gain_ref[...]))[0:1]
    mean = mean[0:1]
    bias = 0.5 * bias_ref[...]

    def activate(raw):
        u = (raw.astype(F32) - mean) * scale + bias
        return (u + u * jnp.tanh(u)).astype(BF16)

    edge_row = iota((EDGE, width), 0)
    edge_voxel = edge_row * TW + jnp.where(edge_row < EDGE // 2, TW - 1, -rows)
    voxel = jnp.concatenate([iota((rows, width), 0), edge_voxel], axis=0)

    def gather(q, blocks=joint):
        some_rows(q, q * joint + joint - blocks, blocks).wait_recv()
        return activate(recv_rows[pl.ds(q * joint, joint)].reshape(width, channels))

    def move(targets, q, arrived):
        return dot((targets == slots_ref[q]).astype(F32).astype(BF16), arrived).astype(BF16)

    half_groups = groups // 2
    quarter_groups = groups // 4
    flip = (odd + 1 - far) % 2

    def group_of(p):
        late = p // half_groups
        low = p % half_groups
        swap = (low // quarter_groups + late * flip) % 2
        return late * half_groups + swap * quarter_groups + low % quarter_groups

    placed_ref[...] = move(voxel, 0, gather(0, joint - 1))

    @pl.loop(1, groups - 1)
    def _(p):
        q = group_of(p)
        placed_ref[...] += move(voxel, q, gather(q))

    grid_rows = tiles // GW
    row_tile = my_tile // GW
    column_tile = my_tile % GW

    def exists(down, right):
        row = row_tile + down
        column = column_tile + right
        return (row >= 0) & (row < grid_rows) & (column >= 0) & (column < GW)

    def halo_copy(e):
        down, right = EDGES[e]
        if e < 2:
            part, source_ref, target_ref = pl.ds(e * (EDGE // 2), EDGE // 2), edge_out, edge_in
        elif e < 4:
            part, source_ref, target_ref = e - 2, face_out, face_in
        else:
            part, source_ref, target_ref = e - 4, corner_out, corner_in
        return pltpu.make_async_remote_copy(
            src_ref=source_ref.at[part],
            dst_ref=target_ref.at[part],
            send_sem=halo_sent.at[e],
            recv_sem=halo_got.at[e],
            device_id=(my_tile + down * GW + right, my_clip),
            device_id_type=MESH,
        )

    def send(e):
        @pl.when(exists(*EDGES[e]))
        def _():
            halo_copy(e).start()

    def receive(e):
        down, right = EDGES[e]

        @pl.when(exists(-down, -right))
        def _():
            halo_copy(e).wait_recv()

    pltpu.make_async_copy(weight_ref, weight_ref, weight_loaded).wait()
    final = group_of(groups - 1)
    tile = placed_ref[...] + move(voxel, final, gather(final))
    edge_out[...] = tile[rows:]
    send(0)
    send(1)
    grid = tile[:rows].reshape(LT, TH, TW, channels)
    for a in range(3):
        volume[2 - a :, 1 : TH + 1, :, a * channels : (a + 1) * channels] = grid[: LT - 2 + a]

    def shifted(product, column):
        taps = [product[:, d * out_width : (d + 1) * out_width] for d in range(3)]
        n = product.shape[0]
        after = jnp.where(column == 0, 0.0, pltpu.roll(taps[0], 1, 0))
        ahead = jnp.where(column == TW - 1, 0.0, pltpu.roll(taps[2], n - 1, 0))
        return after + taps[1] + ahead

    lines = LT * TW
    line_column = iota((lines, out_width), 0) & (TW - 1)
    for f in range(2):
        @pl.when(exists(1 - 2 * f, 0))
        def _():
            b, h = (0, TH) if f == 0 else (2, 1)
            outer = dot(volume[:, h].reshape(lines, 3 * channels), weight_ref[b])
            by_frame = outer.reshape(LT, TW, 3 * out_width)
            for g in range(2):
                w, d = (TW - 1, 0) if g == 0 else (0, 2)
                corner = by_frame[:, w, d * out_width : (d + 1) * out_width]
                corner_out[2 * f + g] = jnp.concatenate(
                    [corner[:, : out_width // 2], corner[:, out_width // 2 :]], axis=0
                )
                send(4 + 2 * f + g)
            face_out[f] = shifted(outer, line_column).astype(BF16)
            send(2 + f)

    plane_column = iota((PLANE, out_width), 0) & (TW - 1)

    out_bias = out_bias_ref[...]

    def frame_sum(t):
        skip = max(0, 2 - t) * channels
        product = None
        for b in range(3):
            slab = volume[t, b : b + TH, :, skip:].reshape(PLANE, 3 * channels - skip)
            term = dot(slab, weight_ref[b, skip:])
            product = term if product is None else product + term
        summed[t] = shifted(product, plane_column) + out_bias

    for t in range(LT):
        frame_sum(t)
    receive(0)
    receive(1)
    edges = edge_in[...].astype(F32)
    edges = jnp.concatenate(
        [edges[n * TH : (n + 1) * TH] for t in range(LT) for n in (t, LT + t)], axis=0
    ).astype(BF16)
    edges = edges.reshape(LT, 2 * TH, channels)
    for a in range(3):
        side[2 - a :, :, a * channels : (a + 1) * channels] = edges[: LT - 2 + a]
    from_left = (iota((EDGE, out_width), 0) & TH) == 0
    line = iota((EDGE, out_width), 0) & (TH - 1)
    beside_in = side[...].reshape(EDGE, 3 * channels)
    taps = []
    for b in range(3):
        taps.append(
            jnp.where(
                from_left,
                dot(beside_in, weight_ref[b, :, :out_width]),
                dot(beside_in, weight_ref[b, :, 2 * out_width :]),
            )
        )
    beside = (
        jnp.where(line == 0, 0.0, pltpu.roll(taps[0], 1, 0))
        + taps[1]
        + jnp.where(line == TH - 1, 0.0, pltpu.roll(taps[2], EDGE - 1, 0))
    )

    strip = TW // 2
    column = iota((strip, out_width), 0)

    def corner_of(i, t):
        return jnp.concatenate([corner_in[i, t : t + 1], corner_in[i, LT + t : LT + t + 1]], axis=1)

    def assemble(lines):
        for t, h in [(t, h) for t in range(LT) for h in lines]:
            for g in range(2):
                n = t * 2 * TH + g * TH + h
                extra = beside[n : n + 1]
                total = summed[t, h * TW + g * strip : h * TW + (g + 1) * strip]
                if h in (0, TH - 1):
                    f = 0 if h == 0 else 1
                    begin = t * TW + g * strip
                    total = total + face_in[f, begin : begin + strip].astype(F32)
                    extra = extra + corner_of(2 * f + g, t)
                total = total + jnp.where(column == g * (strip - 1), extra, 0.0)
                begin = (t * TH + h) * TW + g * strip
                out_ref[begin : begin + strip] = jnp.where(t < live, total, 0.0).astype(BF16)

    assemble(range(1, TH - 1))
    all_metas().wait_send()
    some_rows(0, 1, count - 1).wait_send()
    for e in range(2, 8):
        receive(e)
    assemble((0, TH - 1))

    for e, (down, right) in enumerate(EDGES):
        @pl.when(exists(down, right))
        def _():
            halo_copy(e).wait_send()


def on_device(
    seq_rows, plan_owner, plan_slot, live_frames, norm_gain, norm_bias, conv_weight, conv_bias
):
    rows, channels = seq_rows.shape
    out_width = conv_bias.shape[0]
    tiles = lax.axis_size("tile")
    clips = lax.axis_size("clip")
    count = tiles * clips
    cap = -(-(3 * (rows // count) // 2) // 16) * 16
    joint = joint_of(count, cap)
    dma = pltpu.SemaphoreType.DMA
    decoded = pl.pallas_call(
        functools.partial(decode_kernel, tiles, clips, cap),
        out_shape=pltpu.VMEM((rows, out_width), BF16),
        in_specs=[pl.BlockSpec(memory_space=pltpu.HBM)] * 8,
        out_specs=pl.BlockSpec(memory_space=pltpu.VMEM),
        scratch_shapes=[
            pltpu.SMEM((clips,), jnp.int32),
            pltpu.VMEM((1, rows), jnp.int32),
            pltpu.VMEM((1, rows), jnp.int32),
            pltpu.VMEM((rows, channels), BF16),
            pltpu.VMEM((1, channels), F32),
            pltpu.VMEM((1, channels), F32),
            pltpu.VMEM((1, out_width), F32),
            pltpu.VMEM((3, 3 * channels, 3 * out_width), BF16),
            pltpu.VMEM((count, cap, channels), BF16),
            pltpu.VMEM((count, cap, channels), BF16),
            pltpu.VMEM((count, 1, LANES), F32),
            pltpu.VMEM((count, 1, LANES), F32),
            pltpu.VMEM((count // joint, 1, joint * cap), jnp.int32),
            pltpu.VMEM((rows + EDGE, channels), BF16),
            pltpu.VMEM((LT, TH + 2, TW, 3 * channels), BF16),
            pltpu.VMEM((LT, 2 * TH, 3 * channels), BF16),
            pltpu.VMEM((EDGE, channels), BF16),
            pltpu.VMEM((EDGE, channels), BF16),
            pltpu.VMEM((2, LT * TW, out_width), BF16),
            pltpu.VMEM((2, LT * TW, out_width), BF16),
            pltpu.VMEM((4, 2 * LT, out_width // 2), F32),
            pltpu.VMEM((4, 2 * LT, out_width // 2), F32),
            pltpu.VMEM((LT, PLANE, out_width), F32),
            dma((7,)),
            dma,
            dma,
            dma((count // joint,)),
            dma,
            dma,
            dma((8,)),
            dma((8,)),
        ],
        compiler_params=pltpu.CompilerParams(
            collective_id=0, has_side_effects=True, vmem_limit_bytes=56 << 20
        ),
        name="decode",
    )(
        live_frames,
        plan_owner.reshape(1, rows),
        plan_slot.reshape(1, rows),
        seq_rows,
        norm_gain.reshape(1, channels),
        norm_bias.reshape(1, channels),
        conv_bias.reshape(1, out_width),
        conv_weight.transpose(0, 1, 3, 2, 4).reshape(9, 3 * channels, out_width),
    )

    def finish(held_ref, result_ref, done):
        piece = rows // LT
        copies = [
            pltpu.make_async_copy(
                held_ref.at[pl.ds(t * piece, piece)], result_ref.at[pl.ds(t * piece, piece)], done.at[t]
            )
            for t in range(LT)
        ]
        for copy in copies:
            copy.start()
        for copy in copies:
            copy.wait()

    decoded = pl.pallas_call(
        finish,
        out_shape=jax.ShapeDtypeStruct((rows, out_width), BF16),
        in_specs=[pl.BlockSpec(memory_space=pltpu.VMEM)],
        out_specs=pl.BlockSpec(memory_space=pltpu.HBM),
        scratch_shapes=[dma((LT,))],
        name="finish",
    )(pltpu.with_memory_space_constraint(decoded, pltpu.VMEM))
    return decoded.reshape(1, 1, LT, TH, TW, out_width)


def solution(mesh):
    return jax.shard_map(
        on_device,
        mesh=mesh,
        in_specs=(
            P(("tile", "clip"), None),
            P(("tile", "clip")),
            P(("tile", "clip")),
            P(),
            P(),
            P(),
            P(),
            P(),
        ),
        out_specs=P("clip", "tile", None, None, None, None),
        check_vma=False,
    )
```
